128 devices in a mesh: row: 8 (over y, z_hi), col: 16 (over z_lo, x, core).
Axes of the slice: x: 4, y: 4, z: 4 (z_hi: 2, z_lo: 2; z = z_hi * 2 + z_lo), core: 2. Of those that a mesh axis runs over, the one named last changes fastest.
Arguments:
- measurement_tiling_settings: bfloat16 [65536, 40], P(('row', 'col')), may hold values from -4.875 to 4.875
- dest: int32 [65536], P(('row', 'col')), may hold values from 0 to 65535, as said below
- column_tiling_settings: bfloat16 [32768, 40], P('col'), may hold values from -4.875 to 4.875
- entry_layer_weight: bfloat16 [40, 2048], replicated, may hold values from -1 to 1
- entry_layer_bias: float32 [2048], replicated, may hold values from -3 to 3
- middle_layer_weight: bfloat16 [2048, 2048], replicated, may hold values from -0.1875 to 0.1875
- middle_layer_bias: float32 [2048], replicated, may hold values from -3 to 3
- output_layer_weight: bfloat16 [2048, 256], replicated, may hold values from -0.1875 to 0.1875
- relevance_weight_vector: float32 [256], replicated, may hold values from 0.015625 to 0.03125
- probes: float32 [32768, 64], P('col'), may hold values from -1.3258252 to 1.3258252
Outputs:
- product: float32 [65536, 64], P(('row', 'col'))
The draws below stay inside these ranges and needn't reach their ends.
Inputs may be any that keep to these rules, and one draw needn't show every extreme that they name: dest is a permutation of 0 to 65535, and the measurements held by one device go in equal numbers to the row positions of every device, 4 to each.
All inputs are finite; a program needn't handle non-finite values.
Results may differ from the reference program's by a relative error of at most 0.0088.
Values may be sent and summed in bfloat16 or wider, within the bound.
No kernel may reach another device: no remote copies, remote signals or barrier semaphores. Data moves between devices by JAX's collectives and lax.ppermute only.
A program may use at most 64 MiB of HBM per device.

```python
import math
import jax
import jax.numpy as jnp
from jax import lax

INPUT_DIMENSION = 40
HID = 2048
FEAT = 256
PROBES = 64
R_DEV = 512
KERNEL_ROW_COUNT = 65536
NC = 32768
N_ROW = 8
N_COL = 16


def draw_dest(key, part):
    devices_all = N_ROW * N_COL
    share = R_DEV // devices_all
    first_key, second_key = jax.random.split(jax.random.fold_in(key, 11))
    sigma = jax.vmap(lambda one: jax.random.permutation(one, R_DEV))(jax.random.split(first_key, devices_all))
    tau = jax.vmap(lambda one: jax.random.permutation(one, R_DEV))(jax.random.split(second_key, devices_all))
    target = sigma % devices_all
    sub_slot = sigma // devices_all
    source = jnp.arange(devices_all, dtype=jnp.int32)[:, None]
    slot = source * share + sub_slot
    final = target * R_DEV + tau[target, slot]
    return final.reshape(-1).astype(jnp.int32)


def tiling_values(key, own_key, count):
    values = jnp.clip(1.4 * jax.random.normal(own_key, (count, INPUT_DIMENSION), jnp.float32), -4.875, 4.875)
    return values.astype(jnp.bfloat16)


def draw_measurement_tiling_settings(key, part):
    return tiling_values(key, jax.random.fold_in(key, 21), KERNEL_ROW_COUNT)


def draw_column_tiling_settings(key, part):
    return tiling_values(key, jax.random.fold_in(key, 22), NC)


def levels(key, dims, shards, smallest, largest):
    def one(position, shards_of):
        draws = jax.random.uniform(jax.random.fold_in(jax.random.fold_in(key, 6), position), (shards_of,), jnp.float32, smallest / len(shards), largest / len(shards))
        return jnp.repeat(jnp.exp(draws), dims[position] // shards_of).reshape((-1,) + (1,) * (len(dims) - position - 1))

    gain = one(*shards[0])
    for cut in shards[1:]:
        gain = gain * one(*cut)
    return gain


def gaussian(key, shape, scale, reach, cuts=(), kind=jnp.bfloat16):
    level = levels(key, shape, cuts, -0.22, 0.18) if cuts else 1.0
    values = jax.random.normal(key, shape, jnp.float32) * scale * level
    return jnp.minimum(jnp.maximum(values, -reach), reach).astype(kind)


def setup_inputs(seed: int = 0) -> dict:
    key_of = jax.random.split(jax.random.key(seed), 11)
    return {
        "measurement_tiling_settings": draw_measurement_tiling_settings(jax.random.fold_in(key_of[10], 71), 0),
        "dest": draw_dest(jax.random.fold_in(key_of[10], 71), 0),
        "column_tiling_settings": draw_column_tiling_settings(jax.random.fold_in(key_of[10], 71), 0),
        "entry_layer_weight": gaussian(key_of[3], (INPUT_DIMENSION, HID), INPUT_DIMENSION ** -0.5, 1.0),
        "entry_layer_bias": gaussian(key_of[4], (HID,), 0.5, 3.0, (), jnp.float32),
        "middle_layer_weight": gaussian(key_of[5], (HID, HID), (HID // 2) ** -0.5, 0.1875),
        "middle_layer_bias": gaussian(key_of[6], (HID,), 0.5, 3.0, (), jnp.float32),
        "output_layer_weight": gaussian(key_of[7], (HID, FEAT), (HID // 2) ** -0.5, 0.1875),
        "relevance_weight_vector": jnp.clip(jnp.exp(jax.random.uniform(key_of[8], (FEAT,), jnp.float32, math.log(0.015625), math.log(0.03125))), 0.015625, 0.03125),
        "probes": gaussian(key_of[9], (NC, PROBES), (40.0 / NC ** 0.5), 1.3258252, ((0, 16),), jnp.float32),
    }


def feature_extractor(inputs, entry_layer_weight, entry_layer_bias, middle_layer_weight, middle_layer_bias, output_layer_weight):
    hidden = jnp.maximum(jnp.dot(inputs, entry_layer_weight, preferred_element_type=jnp.float32) + entry_layer_bias, 0.0).astype(jnp.bfloat16)
    hidden = jnp.maximum(jnp.dot(hidden, middle_layer_weight, preferred_element_type=jnp.float32) + middle_layer_bias, 0.0).astype(jnp.bfloat16)
    return jnp.dot(hidden, output_layer_weight, preferred_element_type=jnp.float32).astype(jnp.bfloat16)


def reference(measurement_tiling_settings, dest, column_tiling_settings, entry_layer_weight, entry_layer_bias, middle_layer_weight, middle_layer_bias, output_layer_weight, relevance_weight_vector, probes):
    measurement_feature_rows = feature_extractor(measurement_tiling_settings, entry_layer_weight, entry_layer_bias, middle_layer_weight, middle_layer_bias, output_layer_weight)
    col_feats = feature_extractor(column_tiling_settings, entry_layer_weight, entry_layer_bias, middle_layer_weight, middle_layer_bias, output_layer_weight)
    source_row_index = jnp.zeros((KERNEL_ROW_COUNT,), jnp.int32).at[dest].set(jnp.arange(KERNEL_ROW_COUNT, dtype=jnp.int32))
    row_feature_matrix = measurement_feature_rows[source_row_index]
    scaled = (row_feature_matrix.astype(jnp.float32) * relevance_weight_vector).astype(jnp.bfloat16)
    sq_row = jnp.sum(relevance_weight_vector * jnp.square(row_feature_matrix.astype(jnp.float32)), axis=1)
    sq_col = jnp.sum(relevance_weight_vector * jnp.square(col_feats.astype(jnp.float32)), axis=1)
    block_rows = min(512, KERNEL_ROW_COUNT)
    blocks = KERNEL_ROW_COUNT // block_rows

    def one_block(pieces):
        scaled_rows, sq_rows = pieces
        cross = lax.dot_general(scaled_rows, col_feats, (((1,), (1,)), ((), ())), preferred_element_type=jnp.float32)
        kern = jnp.exp(-0.5 * (sq_rows[:, None] + sq_col[None, :] - 2.0 * cross))
        return jnp.dot(kern, probes, precision=lax.Precision.HIGHEST, preferred_element_type=jnp.float32)

    result = lax.map(one_block, (scaled.reshape(blocks, block_rows, FEAT), sq_row.reshape(blocks, block_rows)))
    return result.reshape(KERNEL_ROW_COUNT, PROBES)
```

```python
import functools

import jax
import jax.numpy as jnp
from jax import lax
from jax.experimental import pallas as pl
from jax.experimental.pallas import tpu as pltpu
from jax.sharding import Mesh, PartitionSpec as P

f32 = jnp.float32
bf16 = jnp.bfloat16
NT = (((1,), (1,)), ((), ()))
TN = (((0,), (0,)), ((), ()))
ALL = ("y", "zh", "zl", "x", "core")
COL = ("zl", "x", "core")
LOG2E = 1.4426950408889634
ROWS = 512
FEAT = 256
UNIT = 512


def dot(a, b):
    return jnp.dot(a, b, preferred_element_type=f32)


def send_kernel(dest_ref, xt_ref, o_ref):
    d_row = dest_ref[...]
    d_f = d_row.astype(f32)
    d_col = jnp.transpose(jnp.broadcast_to(d_f, (128, ROWS)))
    before = jnp.concatenate([d_col] * (ROWS // 128), axis=1) < d_f
    rank = jnp.sum(jnp.where(before, 1.0, 0.0), axis=0, keepdims=True)
    place = lax.broadcasted_iota(jnp.int32, (ROWS, ROWS), 0).astype(f32) == rank
    place = jnp.where(place, 1.0, 0.0).astype(bf16)
    pos = jnp.bitwise_and(d_row, ROWS - 1)
    high = jnp.right_shift(pos, 4).astype(f32)
    low = jnp.bitwise_and(pos, 15).astype(f32)
    line = lax.broadcasted_iota(jnp.int32, (88, ROWS), 0)
    extra = jnp.where(line == 0, high, jnp.where(line == 1, low, 0.0))
    ext = jnp.concatenate([xt_ref[...].astype(f32), extra], axis=0).astype(bf16)
    o_ref[...] = lax.dot_general(place, ext, NT, preferred_element_type=f32).astype(bf16)


def send_rows(dest, x_t):
    return pl.pallas_call(
        send_kernel,
        out_shape=jax.ShapeDtypeStruct((ROWS, 128), bf16),
        name="send_rows",
    )(dest.reshape(1, ROWS), x_t)


def mlp_tail(h1, w2_ref, b2_ref, w3_ref, o_ref, acc, steps):
    i = pl.program_id(0)
    h2 = jnp.maximum(dot(h1[...], w2_ref[...]) + b2_ref[...], 0.0).astype(bf16)
    part = dot(h2, w3_ref[...])

    @pl.when(i == 0)
    def _():
        acc[...] = part

    @pl.when(i > 0)
    def _():
        acc[...] += part

    @pl.when(i == steps - 1)
    def _():
        o_ref[...] = acc[...].astype(bf16)


def col_kernel(y_ref, xt_ref, p_ref, w1_ref, b1_ref, w2_ref, b2_ref, w3_ref, o_ref, q_ref, h1, acc, *, steps):
    @pl.when(pl.program_id(0) == 0)
    def _():
        x = lax.dot_general(xt_ref[...], w1_ref[...], TN, preferred_element_type=f32)
        h1[...] = jnp.maximum(x + b1_ref[...], 0.0).astype(bf16)
        for j in range(8):
            q_ref[j * 64 : (j + 1) * 64, :] = p_ref[:, j * 256 : (j + 1) * 256].astype(bf16)

    mlp_tail(h1, w2_ref, b2_ref, w3_ref, o_ref, acc, steps)


def row_kernel(r_ref, w1_ref, b1_ref, w2_ref, b2_ref, w3_ref, o_ref, h1, acc, *, steps):
    @pl.when(pl.program_id(0) == 0)
    def _():
        got = r_ref[...]
        lane = lax.broadcasted_iota(jnp.int32, (8, 128), 1)
        pick = jnp.where(lane == 40, 16.0, jnp.where(lane == 41, 1.0, 0.0)).astype(bf16)
        pos = lax.dot_general(pick, got, NT, preferred_element_type=f32)[0:1, :]
        place = lax.broadcasted_iota(jnp.int32, (ROWS, ROWS), 0).astype(f32) == pos
        place = jnp.where(place, 1.0, 0.0).astype(bf16)
        x = dot(place, got).astype(bf16)[:, :40]
        h1[...] = jnp.maximum(dot(x, w1_ref[...]) + b1_ref[...], 0.0).astype(bf16)

    mlp_tail(h1, w2_ref, b2_ref, w3_ref, o_ref, acc, steps)


def weight_specs(w1, hid, bn, ft):
    return [
        pl.BlockSpec(w1.shape, lambda i, *_: (0, 0)),
        pl.BlockSpec((1, hid), lambda i, *_: (0, 0)),
        pl.BlockSpec((hid, bn), lambda i, *_: (0, i)),
        pl.BlockSpec((1, bn), lambda i, *_: (0, i)),
        pl.BlockSpec((bn, ft), lambda i, *_: (i, 0)),
    ]


def col_net(y, x_t, p_t, w1, b1, w2, b2, w3, bn=512):
    hid, ft = w2.shape[0], w3.shape[1]
    steps = hid // bn
    spec = pltpu.PrefetchScalarGridSpec(
        num_scalar_prefetch=1,
        grid=(steps,),
        in_specs=[
            pl.BlockSpec((40, UNIT), lambda i, y: (0, y[0])),
            pl.BlockSpec((64, 2048), lambda i, y: (0, 0)),
            *weight_specs(w1, hid, bn, ft),
        ],
        out_specs=[
            pl.BlockSpec((UNIT, ft), lambda i, y: (0, 0)),
            pl.BlockSpec((UNIT, ft), lambda i, y: (0, 0)),
        ],
        scratch_shapes=[pltpu.VMEM((UNIT, hid), bf16), pltpu.VMEM((UNIT, ft), f32)],
    )
    return pl.pallas_call(
        functools.partial(col_kernel, steps=steps),
        grid_spec=spec,
        out_shape=[jax.ShapeDtypeStruct((UNIT, ft), bf16)] * 2,
        name="col_net",
    )(y, x_t, p_t, w1, b1.reshape(1, -1), w2, b2.reshape(1, -1), w3)


def row_net(got, w1, b1, w2, b2, w3, bn=512):
    hid, ft = w2.shape[0], w3.shape[1]
    steps = hid // bn
    return pl.pallas_call(
        functools.partial(row_kernel, steps=steps),
        grid=(steps,),
        in_specs=[pl.BlockSpec((ROWS, 128), lambda i: (0, 0)), *weight_specs(w1, hid, bn, ft)],
        out_specs=pl.BlockSpec((ROWS, ft), lambda i: (0, 0)),
        out_shape=jax.ShapeDtypeStruct((ROWS, ft), bf16),
        scratch_shapes=[pltpu.VMEM((ROWS, hid), bf16), pltpu.VMEM((ROWS, ft), f32)],
        name="row_net",
    )(got, w1, b1.reshape(1, -1), w2, b2.reshape(1, -1), w3)


def rbf_kernel(off_ref, rel_ref, r_ref, *refs, pairs, with_init, bm):
    cols = refs[: 2 * pairs]
    refs = refs[2 * pairs :]
    if with_init:
        init_ref, refs = refs[0], refs[1:]
    o_ref, sc, sqr, sqc, kb, acc = refs
    rel = rel_ref[...]
    rf = r_ref[...].astype(f32)
    sc[...] = (rf * rel).astype(bf16)
    w = rel * rf * rf
    hi = w.astype(bf16)
    lo = (w - hi.astype(f32)).astype(bf16)
    ones = jnp.ones((8, FEAT), bf16)
    sqr[...] = -0.5 * (
        lax.dot_general(ones, hi, NT, preferred_element_type=f32)
        + lax.dot_general(ones, lo, NT, preferred_element_type=f32)
    )
    for p in range(pairs):
        a_ref, b_ref = cols[2 * p], cols[2 * p + 1]
        for u, (ref, at) in enumerate(((a_ref, 0), (a_ref, 1024), (b_ref, 0), (b_ref, 512))):
            start = pl.multiple_of(off_ref[u] * 128 + 512, 128)
            cf = ref[at : at + UNIT, :].astype(f32)
            sqc[...] = jnp.broadcast_to(-0.5 * jnp.sum(rel * cf * cf, axis=1, keepdims=True), sqc.shape)
            for r in range(0, ROWS, bm):
                for b in range(0, UNIT, 256):
                    s = lax.dot_general(
                        ref[at + b : at + b + 256, :], sc[r : r + bm, :], NT, preferred_element_type=f32
                    )
                    q = jnp.concatenate([sqc[b : b + 256, :]] * (bm // 128), axis=1)
                    kb[b : b + 256, r : r + bm] = jnp.exp(s + (q + sqr[0:1, r : r + bm])).astype(bf16)
                t = None
                for b in range(0, UNIT, 256):
                    pr = a_ref[pl.ds(start + (b // 256) * 64, 64), :]
                    part = dot(pr, kb[b : b + 256, r : r + bm])
                    t = part if t is None else t + part
                if p == 0 and u == 0:
                    acc[:, r : r + bm] = t + init_ref[:, r : r + bm] if with_init else t
                else:
                    acc[:, r : r + bm] += t
    o_ref[...] = acc[...].astype(o_ref.dtype)


def rbf(off, rel, rows, col_pairs, init=None, out=f32, bm=256):
    args = [x for pair in col_pairs for x in pair]
    if init is not None:
        args.append(init)
    return pl.pallas_call(
        functools.partial(rbf_kernel, pairs=len(col_pairs), with_init=init is not None, bm=bm),
        in_specs=[pl.BlockSpec(memory_space=pltpu.SMEM)]
        + [pl.BlockSpec(memory_space=pltpu.VMEM)] * (2 + len(args)),
        out_specs=pl.BlockSpec(memory_space=pltpu.VMEM),
        out_shape=jax.ShapeDtypeStruct((64, ROWS), out),
        scratch_shapes=[
            pltpu.VMEM((ROWS, FEAT), bf16),
            pltpu.VMEM((8, ROWS), f32),
            pltpu.VMEM((UNIT, 128), f32),
            pltpu.VMEM((UNIT, ROWS), bf16),
            pltpu.VMEM((64, ROWS), f32),
        ],
        name=f"rbf{len(col_pairs)}",
    )(off, rel, rows, *args)


def ring(shift):
    return [(i, (i + shift) % 4) for i in range(4)]


Z = ("zh", "zl")
SWAP = [(0, 1), (1, 0)]


def per_device(x_m, dest, x_c, w1, b1, w2, b2, w3, rel, probes):
    rel = rel.reshape(1, FEAT)
    y = lax.axis_index("y").astype(jnp.int32)
    own, probe = col_net(y.reshape(1), x_c.T, probes.T, w1, b1, w2, b2, w3)
    u1 = lax.ppermute(own, "y", ring(1))
    u3 = lax.ppermute(own, "y", ring(3))
    u2 = lax.ppermute(own, "y", ring(2))
    off = jnp.stack([y, (y + 3) % 4, (y + 1) % 4, (y + 2) % 4]).astype(jnp.int32)
    sent = send_rows(dest, x_m.T)
    got = lax.all_to_all(sent, ALL, 0, 0, tiled=True)
    feats = row_net(got, w1, b1, w2, b2, w3)
    ca = jnp.concatenate([own, probe, u1], 0)
    cb = jnp.concatenate([u3, u2], 0)
    za = lax.ppermute(ca, Z, ring(1))
    zb = lax.ppermute(cb, Z, ring(3))
    f1 = lax.ppermute(feats, "x", ring(1))
    f3 = lax.ppermute(feats, "x", ring(3))
    f2 = lax.ppermute(feats, "x", ring(2))
    pa = lax.ppermute(ca, "core", SWAP)
    pb = lax.ppermute(cb, "core", SWAP)
    pza = lax.ppermute(za, "core", SWAP)
    pzb = lax.ppermute(zb, "core", SWAP)
    near = [(ca, cb), (pa, pb)]
    far = [(za, zb), (pza, pzb)]
    own1 = rbf(off, rel, feats, near)
    t1 = rbf(off, rel, f1, near)
    t3 = rbf(off, rel, f3, near)
    t1 = rbf(off, rel, f1, far, t1, bf16)
    r1 = lax.ppermute(t1, "x", ring(3))
    t3 = rbf(off, rel, f3, far, t3, bf16)
    r3 = lax.ppermute(t3, "x", ring(1))
    t2 = rbf(off, rel, f2, near + far, None, bf16)
    r2 = lax.ppermute(t2, "x", ring(2))
    mine = rbf(off, rel, feats, far, own1)
    total = mine + r1.astype(f32) + r3.astype(f32) + r2.astype(f32)
    return total.T


def solution(mesh):
    fine = Mesh(mesh.devices.reshape(4, 2, 2, 4, 2), ALL)
    placed = (P(ALL, None), P(ALL), P(COL, None), P(), P(), P(), P(), P(), P(), P(COL, None))
    return jax.shard_map(per_device, mesh=fine, in_specs=placed, out_specs=P(ALL, None), check_vma=False)
```

```python
import functools

import jax
import jax.numpy as jnp
from jax import lax
from jax.experimental import pallas as pl
from jax.experimental.pallas import tpu as pltpu
from jax.sharding import Mesh, PartitionSpec as P


f32 = jnp.float32
bf16 = jnp.bfloat16
NT = (((1,), (1,)), ((), ()))
TN = (((0,), (0,)), ((), ()))
ALL = ("y", "zh", "zl", "x", "core")
COL = ("zl", "x", "core")
LOG2E = 1.4426950408889634
ROWS = 512
FEAT = 256
UNIT = 512
PAIR = 2560


def dot(a, b):
    return jnp.dot(a, b, preferred_element_type=f32)


def send_kernel(dest_ref, xt_ref, o_ref):
    d_row = dest_ref[...]
    d_f = d_row.astype(f32)
    d_col = jnp.transpose(jnp.broadcast_to(d_f, (128, ROWS)))
    before = jnp.concatenate([d_col] * (ROWS // 128), axis=1) < d_f
    rank = jnp.sum(jnp.where(before, 1.0, 0.0), axis=0, keepdims=True)
    place = lax.broadcasted_iota(jnp.int32, (ROWS, ROWS), 0).astype(f32) == rank
    place = jnp.where(place, 1.0, 0.0).astype(bf16)
    pos = jnp.bitwise_and(d_row, ROWS - 1)
    high = jnp.right_shift(pos, 4).astype(f32)
    low = jnp.bitwise_and(pos, 15).astype(f32)
    line = lax.broadcasted_iota(jnp.int32, (88, ROWS), 0)
    extra = jnp.where(line == 0, high, jnp.where(line == 1, low, 0.0))
    ext = jnp.concatenate([xt_ref[...].astype(f32), extra], axis=0).astype(bf16)
    o_ref[...] = lax.dot_general(place, ext, NT, preferred_element_type=f32).astype(bf16)


def send_rows(dest, x_t):
    return pl.pallas_call(
        send_kernel,
        out_shape=jax.ShapeDtypeStruct((ROWS, 128), bf16),
        name="send_rows",
    )(dest.reshape(1, ROWS), x_t)


def mlp_tail(h1, w2_ref, b2_ref, w3_ref, o_ref, acc, steps):
    i = pl.program_id(0)
    h2 = jnp.maximum(dot(h1[...], w2_ref[...]) + b2_ref[...], 0.0).astype(bf16)
    part = dot(h2, w3_ref[...])

    @pl.when(i == 0)
    def _():
        acc[...] = part

    @pl.when(i > 0)
    def _():
        acc[...] += part

    @pl.when(i == steps - 1)
    def _():
        o_ref[...] = acc[...].astype(bf16)


def col_kernel(y_ref, xt_ref, p_ref, w1_ref, b1_ref, w2_ref, b2_ref, w3_ref, o_ref, q_ref, h1, acc, *, steps):
    @pl.when(pl.program_id(0) == 0)
    def _():
        x = lax.dot_general(xt_ref[...], w1_ref[...], TN, preferred_element_type=f32)
        h1[...] = jnp.maximum(x + b1_ref[...], 0.0).astype(bf16)
        for j in range(8):
            q_ref[j * 64 : (j + 1) * 64, :] = p_ref[:, j * 256 : (j + 1) * 256].astype(bf16)

    mlp_tail(h1, w2_ref, b2_ref, w3_ref, o_ref, acc, steps)


def row_kernel(r_ref, w1_ref, b1_ref, w2_ref, b2_ref, w3_ref, o_ref, h1, acc, *, steps):
    @pl.when(pl.program_id(0) == 0)
    def _():
        got = r_ref[...]
        lane = lax.broadcasted_iota(jnp.int32, (8, 128), 1)
        pick = jnp.where(lane == 40, 16.0, jnp.where(lane == 41, 1.0, 0.0)).astype(bf16)
        pos = lax.dot_general(pick, got, NT, preferred_element_type=f32)[0:1, :]
        place = lax.broadcasted_iota(jnp.int32, (ROWS, ROWS), 0).astype(f32) == pos
        place = jnp.where(place, 1.0, 0.0).astype(bf16)
        x = dot(place, got).astype(bf16)[:, :40]
        h1[...] = jnp.maximum(dot(x, w1_ref[...]) + b1_ref[...], 0.0).astype(bf16)

    mlp_tail(h1, w2_ref, b2_ref, w3_ref, o_ref, acc, steps)


def weight_specs(w1, hid, bn, ft):
    return [
        pl.BlockSpec(w1.shape, lambda i, *_: (0, 0)),
        pl.BlockSpec((1, hid), lambda i, *_: (0, 0)),
        pl.BlockSpec((hid, bn), lambda i, *_: (0, i)),
        pl.BlockSpec((1, bn), lambda i, *_: (0, i)),
        pl.BlockSpec((bn, ft), lambda i, *_: (i, 0)),
    ]


def col_net(y, x_t, p_t, w1, b1, w2, b2, w3, bn=512):
    hid, ft = w2.shape[0], w3.shape[1]
    steps = hid // bn
    spec = pltpu.PrefetchScalarGridSpec(
        num_scalar_prefetch=1,
        grid=(steps,),
        in_specs=[
            pl.BlockSpec((40, UNIT), lambda i, y: (0, y[0])),
            pl.BlockSpec((64, 2048), lambda i, y: (0, 0)),
            *weight_specs(w1, hid, bn, ft),
        ],
        out_specs=[
            pl.BlockSpec((UNIT, ft), lambda i, y: (0, 0)),
            pl.BlockSpec((UNIT, ft), lambda i, y: (0, 0)),
        ],
        scratch_shapes=[pltpu.VMEM((UNIT, hid), bf16), pltpu.VMEM((UNIT, ft), f32)],
    )
    return pl.pallas_call(
        functools.partial(col_kernel, steps=steps),
        grid_spec=spec,
        out_shape=[jax.ShapeDtypeStruct((UNIT, ft), bf16)] * 2,
        name="col_net",
    )(y, x_t, p_t, w1, b1.reshape(1, -1), w2, b2.reshape(1, -1), w3)


def row_net(got, w1, b1, w2, b2, w3, bn=512):
    hid, ft = w2.shape[0], w3.shape[1]
    steps = hid // bn
    return pl.pallas_call(
        functools.partial(row_kernel, steps=steps),
        grid=(steps,),
        in_specs=[pl.BlockSpec((ROWS, 128), lambda i: (0, 0)), *weight_specs(w1, hid, bn, ft)],
        out_specs=pl.BlockSpec((ROWS, ft), lambda i: (0, 0)),
        out_shape=jax.ShapeDtypeStruct((ROWS, ft), bf16),
        scratch_shapes=[pltpu.VMEM((ROWS, hid), bf16), pltpu.VMEM((ROWS, ft), f32)],
        name="row_net",
    )(got, w1, b1.reshape(1, -1), w2, b2.reshape(1, -1), w3)


def rbf_kernel(off_ref,rel_ref,*refs,nr,pairs,with_init,bm,cs,ug):
    rows=refs[:nr]; refs=refs[nr:]
    cols=refs[:2*pairs]; refs=refs[2*pairs:]
    if with_init: init_ref,refs=refs[0],refs[1:]
    outs=refs[:nr]; refs=refs[nr:]
    sc,sqr,cv,sv,kv,acc,sem=refs
    m=nr*ROWS

    def copies(p,a,b):
        return (pltpu.make_async_copy(a,cv.at[pl.ds(pl.multiple_of(p*PAIR,PAIR),1536)],sem.at[2*p]),
                pltpu.make_async_copy(b,cv.at[pl.ds(pl.multiple_of(p*PAIR+1536,512),1024)],sem.at[2*p+1]))

    for p in range(pairs):
        for c in copies(p,cols[2*p],cols[2*p+1]): c.start()
    rel=rel_ref[...]
    ones=jnp.ones((8,FEAT),bf16)
    for j in range(nr):
        at=slice(j*ROWS,(j+1)*ROWS)
        rf=rows[j][...].astype(f32)
        sc[at,:]=(rf*(rel*LOG2E)).astype(bf16)
        w=rel*rf*rf
        hi=w.astype(bf16); lo=(w-hi.astype(f32)).astype(bf16)
        sqr[:,at]=(-0.5*LOG2E)*(lax.dot_general(ones,hi,NT,preferred_element_type=f32)+lax.dot_general(ones,lo,NT,preferred_element_type=f32))
        acc[:,at]=init_ref[...] if with_init else jnp.zeros((64,ROWS),f32)

    def body(p,_):
        for c in copies(p,cols[0],cols[1]): c.wait()
        starts=[pl.multiple_of(p*PAIR+(0 if u==0 else 512+u*512),512) for u in range(4)]
        for u0 in range(0,4,ug):
            us=range(u0,u0+ug)
            for u in us:
                c=cv[pl.ds(starts[u],UNIT),:].astype(f32)
                sv[u*UNIT:(u+1)*UNIT,:]=jnp.broadcast_to((-0.5*LOG2E)*jnp.sum(rel*c*c,axis=1,keepdims=True),(UNIT,128))
            prs=[]
            for u in us:
                st=pl.multiple_of(p*PAIR+512+off_ref[u]*128,128)
                prs+=[cv[pl.ds(st,64),:],cv[pl.ds(st+64,64),:]]
            pr=jnp.concatenate(prs,axis=1)
            for r in range(0,m,bm):
                for u in us:
                    for b in range(0,UNIT,cs):
                        s=lax.dot_general(cv[pl.ds(starts[u]+b,cs),:],sc[r:r+bm,:],NT,preferred_element_type=f32)
                        q=sv[u*UNIT+b:u*UNIT+b+cs,:]
                        q=jnp.concatenate([q]*(bm//128),axis=1)
                        kv[u*UNIT+b:u*UNIT+b+cs,r:r+bm]=jnp.exp2(s+(q+sqr[0:1,r:r+bm])).astype(bf16)
                acc[:,r:r+bm]+=jnp.dot(pr,kv[u0*UNIT:(u0+ug)*UNIT,r:r+bm],preferred_element_type=f32)
        return 0

    lax.fori_loop(0,pairs,body,0)
    for j in range(nr): outs[j][...]=acc[:,j*ROWS:(j+1)*ROWS].astype(outs[j].dtype)


def rbf(off,rel,rows,pairs,init=None,out=f32,bm=256,cs=512,ug=4):
    nr=len(rows)
    args=list(rows)+[x for p in pairs for x in p]+([init] if init is not None else [])
    V=pl.BlockSpec(memory_space=pltpu.VMEM); A=pl.BlockSpec(memory_space=pl.ANY)
    npairs=len(pairs); m=nr*ROWS
    return pl.pallas_call(functools.partial(rbf_kernel,nr=nr,pairs=npairs,with_init=init is not None,bm=bm,cs=cs,ug=ug),
        in_specs=[pl.BlockSpec(memory_space=pltpu.SMEM),V]+[V]*nr+[A]*(2*npairs)+([V] if init is not None else []),
        out_specs=[V]*nr,out_shape=[jax.ShapeDtypeStruct((64,ROWS),out)]*nr,
        scratch_shapes=[pltpu.VMEM((m,FEAT),bf16),pltpu.VMEM((8,m),f32),pltpu.VMEM((npairs*PAIR,FEAT),bf16),pltpu.VMEM((2048,128),f32),
          pltpu.VMEM((2048,m),bf16),pltpu.VMEM((64,m),f32),pltpu.SemaphoreType.DMA((2*npairs,))])(off,rel,*args)


def ring(shift):
    return [(i, (i + shift) % 4) for i in range(4)]


Z = ("zh", "zl")
SWAP = [(0, 1), (1, 0)]


def steps(x_m, dest, x_c, w1, b1, w2, b2, w3, rel, probes):
    rel = rel.reshape(1, FEAT)
    y = lax.axis_index("y").astype(jnp.int32)
    off = jnp.stack([y, (y + 3) % 4, (y + 1) % 4, (y + 2) % 4]).astype(jnp.int32)
    sent = send_rows(dest, x_m.T)
    own, probe = col_net(y.reshape(1), x_c.T, probes.T, w1, b1, w2, b2, w3)
    sent, own = lax.optimization_barrier((sent, own))
    u1 = lax.ppermute(own, "y", ring(1))
    u3 = lax.ppermute(own, "y", ring(3))
    u2 = lax.ppermute(own, "y", ring(2))
    got = lax.all_to_all(sent, ALL, 0, 0, tiled=True)
    u1, u3, u2, got = lax.optimization_barrier((u1, u3, u2, got))
    feats = row_net(got, w1, b1, w2, b2, w3)
    ca = jnp.concatenate([own, probe, u1], 0)
    cb = jnp.concatenate([u3, u2], 0)
    za = lax.ppermute(ca, Z, ring(1))
    zb = lax.ppermute(cb, Z, ring(3))
    pa = lax.ppermute(ca, "core", SWAP)
    pb = lax.ppermute(cb, "core", SWAP)
    f1 = lax.ppermute(feats, "x", ring(1))
    f3 = lax.ppermute(feats, "x", ring(3))
    f2 = lax.ppermute(feats, "x", ring(2))
    near = [(ca, cb), (pa, pb)]
    (first,) = rbf(off, rel, [feats], near, bm=512)
    za, zb, first = lax.optimization_barrier((za, zb, first))
    pza = lax.ppermute(za, "core", SWAP)
    pzb = lax.ppermute(zb, "core", SWAP)
    far = [(za, zb), (pza, pzb)]
    t1, t3 = rbf(off, rel, [f1, f3], near + far, out=bf16)
    r1 = lax.ppermute(t1, "x", ring(3))
    r3 = lax.ppermute(t3, "x", ring(1))
    (t2,) = rbf(off, rel, [f2], near + far, out=bf16, bm=512)
    r2 = lax.ppermute(t2, "x", ring(2))
    (mine,) = rbf(off, rel, [feats], far, first, bm=512)
    total = mine + r1.astype(f32) + r3.astype(f32) + r2.astype(f32)
    return total.T


def solution(mesh):
    fine = Mesh(mesh.devices.reshape(4, 2, 2, 4, 2), ALL)
    placed = (P(ALL, None), P(ALL), P(COL, None), P(), P(), P(), P(), P(), P(), P(COL, None))
    return jax.shard_map(steps, mesh=fine, in_specs=placed, out_specs=P(ALL, None), check_vma=False)
```

```python
import functools

import jax
import jax.numpy as jnp
from jax import lax
from jax.experimental import pallas as pl
from jax.experimental.pallas import tpu as pltpu
from jax.sharding import Mesh, PartitionSpec as P


f32 = jnp.float32
bf16 = jnp.bfloat16
NT = (((1,), (1,)), ((), ()))
TN = (((0,), (0,)), ((), ()))
ALL = ("y", "zh", "zl", "x", "core")
COL = ("zl", "x", "core")
LOG2E = 1.4426950408889634
ROWS = 512
FEAT = 256
UNIT = 512
PAIR = 2560


def dot(a, b):
    return jnp.dot(a, b, preferred_element_type=f32)


CHUNK = 512


def weight_copies(w2_ref, w3_ref, w2_v, w3_v, sem):
    chunks = w2_v.shape[0]
    for c in range(chunks):
        pltpu.make_async_copy(w2_ref.at[:, pl.ds(c * CHUNK, CHUNK)], w2_v.at[c], sem.at[c]).start()
        if c == 0:
            pltpu.make_async_copy(w3_ref, w3_v, sem.at[chunks]).start()


def last_layers(w2_ref, b2_ref, w3_ref, o_ref, h1, w2_v, w3_v, acc, sem):
    chunks = w2_v.shape[0]

    def chunk(c):
        pltpu.make_async_copy(w2_ref.at[:, pl.ds(0, CHUNK)], w2_v.at[c], sem.at[c]).wait()
        at = pl.multiple_of(c * CHUNK, CHUNK)
        h2 = jnp.maximum(dot(h1[...], w2_v[c]) + b2_ref[:, pl.ds(at, CHUNK)], 0.0).astype(bf16)
        return h2, at

    h2, _ = chunk(0)
    pltpu.make_async_copy(w3_ref, w3_v, sem.at[chunks]).wait()
    acc[...] = dot(h2, w3_v[0:CHUNK, :])

    def body(c, _):
        h2, at = chunk(c)
        acc[...] += dot(h2, w3_v[pl.ds(at, CHUNK), :])
        return 0

    lax.fori_loop(1, chunks, body, 0)
    o_ref[...] = acc[...].astype(bf16)


def reorder(dest_ref, xt_ref, o_ref):
    d_row = dest_ref[...]
    d_f = d_row.astype(f32)
    d_col = jnp.transpose(jnp.broadcast_to(d_f, (128, ROWS)))
    before = jnp.concatenate([d_col] * (ROWS // 128), axis=1) < d_f
    rank = jnp.sum(jnp.where(before, 1.0, 0.0), axis=0, keepdims=True)
    place = lax.broadcasted_iota(jnp.int32, (ROWS, ROWS), 0).astype(f32) == rank
    place = jnp.where(place, 1.0, 0.0).astype(bf16)
    pos = jnp.bitwise_and(d_row, ROWS - 1)
    high = jnp.right_shift(pos, 4).astype(f32)
    low = jnp.bitwise_and(pos, 15).astype(f32)
    line = lax.broadcasted_iota(jnp.int32, (88, ROWS), 0)
    extra = jnp.where(line == 0, high, jnp.where(line == 1, low, 0.0))
    ext = jnp.concatenate([xt_ref[...].astype(f32), extra], axis=0).astype(bf16)
    o_ref[...] = lax.dot_general(place, ext, NT, preferred_element_type=f32).astype(bf16)


def front_kernel(
    y_ref, dest_ref, xm_ref, xc_ref, p_ref, w1_ref, b1_ref, w2_ref, b2_ref, w3_ref,
    s_ref, o_ref, q_ref, h1, w2_v, w3_v, acc, sem,
):
    weight_copies(w2_ref, w3_ref, w2_v, w3_v, sem)
    reorder(dest_ref, xm_ref, s_ref)
    for j in range(8):
        q_ref[j * 64 : (j + 1) * 64, :] = p_ref[:, j * 256 : (j + 1) * 256].astype(bf16)
    xc = xc_ref[:, pl.ds(pl.multiple_of(y_ref[0] * UNIT, UNIT), UNIT)]
    x = lax.dot_general(xc, w1_ref[...], TN, preferred_element_type=f32)
    h1[...] = jnp.maximum(x + b1_ref[...], 0.0).astype(bf16)
    last_layers(w2_ref, b2_ref, w3_ref, o_ref, h1, w2_v, w3_v, acc, sem)


def row_kernel(r_ref, w1_ref, b1_ref, w2_ref, b2_ref, w3_ref, o_ref, h1, w2_v, w3_v, acc, sem):
    weight_copies(w2_ref, w3_ref, w2_v, w3_v, sem)
    got = r_ref[...]
    lane = lax.broadcasted_iota(jnp.int32, (8, 128), 1)
    pick = jnp.where(lane == 40, 16.0, jnp.where(lane == 41, 1.0, 0.0)).astype(bf16)
    pos = lax.dot_general(pick, got, NT, preferred_element_type=f32)[0:1, :]
    place = lax.broadcasted_iota(jnp.int32, (ROWS, ROWS), 0).astype(f32) == pos
    place = jnp.where(place, 1.0, 0.0).astype(bf16)
    x = dot(place, got).astype(bf16)[:, :40]
    h1[...] = jnp.maximum(dot(x, w1_ref[...]) + b1_ref[...], 0.0).astype(bf16)
    last_layers(w2_ref, b2_ref, w3_ref, o_ref, h1, w2_v, w3_v, acc, sem)


VM = pl.BlockSpec(memory_space=pltpu.VMEM)
SM = pl.BlockSpec(memory_space=pltpu.SMEM)
HB = pl.BlockSpec(memory_space=pltpu.HBM)
LIMIT = pltpu.CompilerParams(vmem_limit_bytes=30 * 2**20)
WEIGHT_SPECS = [VM, VM, HB, VM, HB]


def net_scratch(m, hid, ft):
    return [
        pltpu.VMEM((m, hid), bf16),
        pltpu.VMEM((hid // CHUNK, hid, CHUNK), bf16),
        pltpu.VMEM((hid, ft), bf16),
        pltpu.VMEM((m, ft), f32),
        pltpu.SemaphoreType.DMA((hid // CHUNK + 1,)),
    ]


def front(y, dest, x_m, x_c, p_t, w1, b1, w2, b2, w3):
    hid, ft = w2.shape[0], w3.shape[1]
    return pl.pallas_call(
        front_kernel,
        in_specs=[SM, VM, VM, VM, VM, *WEIGHT_SPECS],
        out_specs=[VM] * 3,
        out_shape=[
            jax.ShapeDtypeStruct((ROWS, 128), bf16),
            jax.ShapeDtypeStruct((UNIT, ft), bf16),
            jax.ShapeDtypeStruct((UNIT, ft), bf16),
        ],
        scratch_shapes=net_scratch(UNIT, hid, ft),
        name="front",
    )(y, dest.reshape(1, ROWS), x_m, x_c, p_t, w1, b1.reshape(1, -1), w2, b2.reshape(1, -1), w3)


def row_net(got, w1, b1, w2, b2, w3):
    hid, ft = w2.shape[0], w3.shape[1]
    return pl.pallas_call(
        row_kernel,
        in_specs=[VM, *WEIGHT_SPECS],
        out_specs=VM,
        out_shape=jax.ShapeDtypeStruct((ROWS, ft), bf16),
        scratch_shapes=net_scratch(ROWS, hid, ft),
        name="row_net",
    )(got, w1, b1.reshape(1, -1), w2, b2.reshape(1, -1), w3)


def rbf_kernel(off_ref,rel_ref,*refs,nr,pairs,with_init,bm,cs,ug):
    rows=refs[:nr]; refs=refs[nr:]
    cols=refs[:2*pairs]; refs=refs[2*pairs:]
    if with_init: init_ref,refs=refs[0],refs[1:]
    outs=refs[:nr]; refs=refs[nr:]
    sc,sqr,cv,sv,kv,acc,sem=refs
    m=nr*ROWS

    def copies(p,a,b):
        return (pltpu.make_async_copy(a,cv.at[pl.ds(pl.multiple_of(p*PAIR,PAIR),1536)],sem.at[2*p]),
                pltpu.make_async_copy(b,cv.at[pl.ds(pl.multiple_of(p*PAIR+1536,512),1024)],sem.at[2*p+1]))

    for p in range(pairs):
        for c in copies(p,cols[2*p],cols[2*p+1]): c.start()
    rel=rel_ref[...]
    ones=jnp.ones((8,FEAT),bf16)
    for j in range(nr):
        at=slice(j*ROWS,(j+1)*ROWS)
        rf=rows[j][...].astype(f32)
        sc[at,:]=(rf*(rel*LOG2E)).astype(bf16)
        w=rel*rf*rf
        hi=w.astype(bf16); lo=(w-hi.astype(f32)).astype(bf16)
        sqr[:,at]=(-0.5*LOG2E)*(lax.dot_general(ones,hi,NT,preferred_element_type=f32)+lax.dot_general(ones,lo,NT,preferred_element_type=f32))
        acc[:,at]=init_ref[...] if with_init else jnp.zeros((64,ROWS),f32)

    def body(p,_):
        for c in copies(p,cols[0],cols[1]): c.wait()
        starts=[pl.multiple_of(p*PAIR+(0 if u==0 else 512+u*512),512) for u in range(4)]
        for u0 in range(0,4,ug):
            us=range(u0,u0+ug)
            for u in us:
                c=cv[pl.ds(starts[u],UNIT),:].astype(f32)
                sv[u*UNIT:(u+1)*UNIT,:]=jnp.broadcast_to((-0.5*LOG2E)*jnp.sum(rel*c*c,axis=1,keepdims=True),(UNIT,128))
            prs=[]
            for u in us:
                st=pl.multiple_of(p*PAIR+512+off_ref[u]*128,128)
                prs+=[cv[pl.ds(st,64),:],cv[pl.ds(st+64,64),:]]
            pr=jnp.concatenate(prs,axis=1)
            for r in range(0,m,bm):
                for u in us:
                    for b in range(0,UNIT,cs):
                        s=lax.dot_general(cv[pl.ds(starts[u]+b,cs),:],sc[r:r+bm,:],NT,preferred_element_type=f32)
                        q=sv[u*UNIT+b:u*UNIT+b+cs,:]
                        q=jnp.concatenate([q]*(bm//128),axis=1)
                        kv[u*UNIT+b:u*UNIT+b+cs,r:r+bm]=jnp.exp2(s+(q+sqr[0:1,r:r+bm])).astype(bf16)
                acc[:,r:r+bm]+=jnp.dot(pr,kv[u0*UNIT:(u0+ug)*UNIT,r:r+bm],preferred_element_type=f32)
        return 0

    lax.fori_loop(0,pairs,body,0)
    for j in range(nr): outs[j][...]=acc[:,j*ROWS:(j+1)*ROWS].astype(outs[j].dtype)


def rbf(off,rel,rows,pairs,init=None,out=f32,bm=256,cs=512,ug=4):
    nr=len(rows)
    args=list(rows)+[x for p in pairs for x in p]+([init] if init is not None else [])
    V = VM
    npairs=len(pairs); m=nr*ROWS
    return pl.pallas_call(functools.partial(rbf_kernel,nr=nr,pairs=npairs,with_init=init is not None,bm=bm,cs=cs,ug=ug),
        in_specs=[SM,V]+[V]*nr+[V]*(2*npairs)+([V] if init is not None else []),
        out_specs=[V]*nr,out_shape=[jax.ShapeDtypeStruct((64,ROWS),out)]*nr,
        scratch_shapes=[pltpu.VMEM((m,FEAT),bf16),pltpu.VMEM((8,m),f32),pltpu.VMEM((npairs*PAIR,FEAT),bf16),pltpu.VMEM((2048,128),f32),
          pltpu.VMEM((2048,m),bf16),pltpu.VMEM((64,m),f32),pltpu.SemaphoreType.DMA((2*npairs,))],
        compiler_params=LIMIT)(off,rel,*args)


def ring(shift):
    return [(i, (i + shift) % 4) for i in range(4)]


Z = ("zh", "zl")
SWAP = [(0, 1), (1, 0)]


def steps(x_m, dest, x_c, w1, b1, w2, b2, w3, rel, probes):
    rel = rel.reshape(1, FEAT)
    y = lax.axis_index("y").astype(jnp.int32)
    off = jnp.stack([y, (y + 3) % 4, (y + 1) % 4, (y + 2) % 4]).astype(jnp.int32)
    sent, own, probe = front(y.reshape(1), dest, x_m.T, x_c.T, probes.T, w1, b1, w2, b2, w3)
    u1 = lax.ppermute(own, "y", ring(1))
    u3 = lax.ppermute(own, "y", ring(3))
    u2 = lax.ppermute(own, "y", ring(2))
    got = lax.all_to_all(sent, ALL, 0, 0, tiled=True)
    u1, u3, u2, got = lax.optimization_barrier((u1, u3, u2, got))
    feats = row_net(got, w1, b1, w2, b2, w3)
    ca = jnp.concatenate([own, probe, u1], 0)
    cb = jnp.concatenate([u3, u2], 0)
    za = lax.ppermute(ca, Z, ring(1))
    zb = lax.ppermute(cb, Z, ring(3))
    pa = lax.ppermute(ca, "core", SWAP)
    pb = lax.ppermute(cb, "core", SWAP)
    f1 = lax.ppermute(feats, "x", ring(1))
    f3 = lax.ppermute(feats, "x", ring(3))
    f2 = lax.ppermute(feats, "x", ring(2))
    near = [(ca, cb), (pa, pb)]
    (first,) = rbf(off, rel, [feats], near, bm=512)
    za, zb, first = lax.optimization_barrier((za, zb, first))
    pza = lax.ppermute(za, "core", SWAP)
    pzb = lax.ppermute(zb, "core", SWAP)
    far = [(za, zb), (pza, pzb)]
    t1, t3 = rbf(off, rel, [f1, f3], near + far, out=bf16)
    r1 = lax.ppermute(t1, "x", ring(3))
    r3 = lax.ppermute(t3, "x", ring(1))
    (t2,) = rbf(off, rel, [f2], near + far, out=bf16, bm=512)
    r2 = lax.ppermute(t2, "x", ring(2))
    (mine,) = rbf(off, rel, [feats], far, first, bm=512)
    total = mine + r1.astype(f32) + r3.astype(f32) + r2.astype(f32)
    return total.T


def solution(mesh):
    fine = Mesh(mesh.devices.reshape(4, 2, 2, 4, 2), ALL)
    placed = (P(ALL, None), P(ALL), P(COL, None), P(), P(), P(), P(), P(), P(), P(COL, None))
    return jax.shard_map(steps, mesh=fine, in_specs=placed, out_specs=P(ALL, None), check_vma=False)
```

```python
import functools

import jax
import jax.numpy as jnp
from jax import lax
from jax.experimental import pallas as pl
from jax.experimental.pallas import tpu as pltpu
from jax.sharding import Mesh, PartitionSpec as P


f32 = jnp.float32
bf16 = jnp.bfloat16
NT = (((1,), (1,)), ((), ()))
TN = (((0,), (0,)), ((), ()))
ALL = ("y", "zh", "zl", "x", "core")
COL = ("zl", "x", "core")
LOG2E = 1.4426950408889634
ROWS = 512
FEAT = 256
UNIT = 512
PAIR = 2560


def dot(a, b):
    return jnp.dot(a, b, preferred_element_type=f32)


CHUNK = 512


def weight_copies(w2_ref, w3_ref, w2_v, w3_v, sem):
    chunks = w2_v.shape[0]
    for c in range(chunks):
        pltpu.make_async_copy(w2_ref.at[:, pl.ds(c * CHUNK, CHUNK)], w2_v.at[c], sem.at[c]).start()
        if c == 0:
            pltpu.make_async_copy(w3_ref, w3_v, sem.at[chunks]).start()


def last_layers(w2_ref, b2_ref, w3_ref, o_ref, h1, w2_v, w3_v, acc, sem):
    chunks = w2_v.shape[0]

    def chunk(c):
        pltpu.make_async_copy(w2_ref.at[:, pl.ds(0, CHUNK)], w2_v.at[c], sem.at[c]).wait()
        at = pl.multiple_of(c * CHUNK, CHUNK)
        h2 = jnp.maximum(dot(h1[...], w2_v[c]) + b2_ref[:, pl.ds(at, CHUNK)], 0.0).astype(bf16)
        return h2, at

    h2, _ = chunk(0)
    pltpu.make_async_copy(w3_ref, w3_v, sem.at[chunks]).wait()
    acc[...] = dot(h2, w3_v[0:CHUNK, :])

    def body(c, _):
        h2, at = chunk(c)
        acc[...] += dot(h2, w3_v[pl.ds(at, CHUNK), :])
        return 0

    lax.fori_loop(1, chunks, body, 0)
    o_ref[...] = acc[...].astype(bf16)


def reorder(dest_ref, xt_ref, o_ref):
    d_row = dest_ref[...]
    d_f = d_row.astype(f32)
    d_col = jnp.transpose(jnp.broadcast_to(d_f, (128, ROWS)))
    before = jnp.concatenate([d_col] * (ROWS // 128), axis=1) < d_f
    rank = jnp.sum(jnp.where(before, 1.0, 0.0), axis=0, keepdims=True)
    place = lax.broadcasted_iota(jnp.int32, (ROWS, ROWS), 0).astype(f32) == rank
    place = jnp.where(place, 1.0, 0.0).astype(bf16)
    pos = jnp.bitwise_and(d_row, ROWS - 1)
    high = jnp.right_shift(pos, 4).astype(f32)
    low = jnp.bitwise_and(pos, 15).astype(f32)
    line = lax.broadcasted_iota(jnp.int32, (88, ROWS), 0)
    extra = jnp.where(line == 0, high, jnp.where(line == 1, low, 0.0))
    ext = jnp.concatenate([xt_ref[...].astype(f32), extra], axis=0).astype(bf16)
    o_ref[...] = lax.dot_general(place, ext, NT, preferred_element_type=f32).astype(bf16)


def front_kernel(
    y_ref, dest_ref, xm_ref, xc_ref, p_ref, w1_ref, b1_ref, w2_ref, b2_ref, w3_ref,
    s_ref, o_ref, q_ref, h1, w2_v, w3_v, acc, sem,
):
    weight_copies(w2_ref, w3_ref, w2_v, w3_v, sem)
    reorder(dest_ref, xm_ref, s_ref)
    for j in range(8):
        q_ref[j * 64 : (j + 1) * 64, :] = p_ref[:, j * 256 : (j + 1) * 256].astype(bf16)
    xc = xc_ref[:, pl.ds(pl.multiple_of(y_ref[0] * UNIT, UNIT), UNIT)]
    x = lax.dot_general(xc, w1_ref[...], TN, preferred_element_type=f32)
    h1[...] = jnp.maximum(x + b1_ref[...], 0.0).astype(bf16)
    last_layers(w2_ref, b2_ref, w3_ref, o_ref, h1, w2_v, w3_v, acc, sem)


def row_kernel(r_ref, w1_ref, b1_ref, w2_ref, b2_ref, w3_ref, o_ref, h1, w2_v, w3_v, acc, sem):
    weight_copies(w2_ref, w3_ref, w2_v, w3_v, sem)
    got = r_ref[...]
    lane = lax.broadcasted_iota(jnp.int32, (8, 128), 1)
    pick = jnp.where(lane == 40, 16.0, jnp.where(lane == 41, 1.0, 0.0)).astype(bf16)
    pos = lax.dot_general(pick, got, NT, preferred_element_type=f32)[0:1, :]
    place = lax.broadcasted_iota(jnp.int32, (ROWS, ROWS), 0).astype(f32) == pos
    place = jnp.where(place, 1.0, 0.0).astype(bf16)
    x = dot(place, got).astype(bf16)[:, :40]
    h1[...] = jnp.maximum(dot(x, w1_ref[...]) + b1_ref[...], 0.0).astype(bf16)
    last_layers(w2_ref, b2_ref, w3_ref, o_ref, h1, w2_v, w3_v, acc, sem)


VM = pl.BlockSpec(memory_space=pltpu.VMEM)
SM = pl.BlockSpec(memory_space=pltpu.SMEM)
HB = pl.BlockSpec(memory_space=pltpu.HBM)
LIMIT = pltpu.CompilerParams(vmem_limit_bytes=30 * 2**20)
WEIGHT_SPECS = [VM, VM, HB, VM, HB]


def net_scratch(m, hid, ft):
    return [
        pltpu.VMEM((m, hid), bf16),
        pltpu.VMEM((hid // CHUNK, hid, CHUNK), bf16),
        pltpu.VMEM((hid, ft), bf16),
        pltpu.VMEM((m, ft), f32),
        pltpu.SemaphoreType.DMA((hid // CHUNK + 1,)),
    ]


def front(y, dest, x_m, x_c, p_t, w1, b1, w2, b2, w3):
    hid, ft = w2.shape[0], w3.shape[1]
    return pl.pallas_call(
        front_kernel,
        in_specs=[SM, VM, VM, VM, VM, *WEIGHT_SPECS],
        out_specs=[VM] * 3,
        out_shape=[
            jax.ShapeDtypeStruct((ROWS, 128), bf16),
            jax.ShapeDtypeStruct((UNIT, ft), bf16),
            jax.ShapeDtypeStruct((UNIT, ft), bf16),
        ],
        scratch_shapes=net_scratch(UNIT, hid, ft),
        name="front",
    )(y, dest.reshape(1, ROWS), x_m, x_c, p_t, w1, b1.reshape(1, -1), w2, b2.reshape(1, -1), w3)


def row_net(got, w1, b1, w2, b2, w3):
    hid, ft = w2.shape[0], w3.shape[1]
    return pl.pallas_call(
        row_kernel,
        in_specs=[VM, *WEIGHT_SPECS],
        out_specs=VM,
        out_shape=jax.ShapeDtypeStruct((ROWS, ft), bf16),
        scratch_shapes=net_scratch(ROWS, hid, ft),
        name="row_net",
    )(got, w1, b1.reshape(1, -1), w2, b2.reshape(1, -1), w3)


def rbf_kernel(off_ref,rel_ref,*refs,nr,pairs,with_init,bm,cs,ug):
    rows=refs[:nr]; refs=refs[nr:]
    cols=refs[:2*pairs]; refs=refs[2*pairs:]
    if with_init: init_ref,refs=refs[0],refs[1:]
    outs=refs[:nr]; refs=refs[nr:]
    sc,sqr,cv,sv,kv,acc,sem=refs
    m=nr*ROWS

    def copies(p,a,b):
        return (pltpu.make_async_copy(a,cv.at[pl.ds(pl.multiple_of(p*PAIR,PAIR),1280)],sem.at[2*p]),
                pltpu.make_async_copy(b,cv.at[pl.ds(pl.multiple_of(p*PAIR+1280,256),1280)],sem.at[2*p+1]))

    for p in range(pairs):
        for c in copies(p,cols[2*p],cols[2*p+1]): c.start()
    rel=rel_ref[...]
    ones=jnp.ones((8,FEAT),bf16)
    for j in range(nr):
        at=slice(j*ROWS,(j+1)*ROWS)
        rf=rows[j][...].astype(f32)
        sc[at,:]=(rf*(rel*LOG2E)).astype(bf16)
        w=rel*rf*rf
        hi=w.astype(bf16); lo=(w-hi.astype(f32)).astype(bf16)
        sqr[:,at]=(-0.5*LOG2E)*(lax.dot_general(ones,hi,NT,preferred_element_type=f32)+lax.dot_general(ones,lo,NT,preferred_element_type=f32))
        acc[:,at]=init_ref[...] if with_init else jnp.zeros((64,ROWS),f32)

    def body(p,_):
        for c in copies(p,cols[0],cols[1]): c.wait()
        starts=[pl.multiple_of(p*PAIR+(0 if u==0 else 512+u*512),512) for u in range(4)]
        for u0 in range(0,4,ug):
            us=range(u0,u0+ug)
            for u in us:
                c=cv[pl.ds(starts[u],UNIT),:].astype(f32)
                sv[u*UNIT:(u+1)*UNIT,:]=jnp.broadcast_to((-0.5*LOG2E)*jnp.sum(rel*c*c,axis=1,keepdims=True),(UNIT,128))
            prs=[]
            for u in us:
                st=pl.multiple_of(p*PAIR+512+off_ref[u]*128,128)
                prs+=[cv[pl.ds(st,64),:],cv[pl.ds(st+64,64),:]]
            pr=jnp.concatenate(prs,axis=1)
            for r in range(0,m,bm):
                for u in us:
                    for b in range(0,UNIT,cs):
                        s=lax.dot_general(cv[pl.ds(starts[u]+b,cs),:],sc[r:r+bm,:],NT,preferred_element_type=f32)
                        q=sv[u*UNIT+b:u*UNIT+b+cs,:]
                        q=jnp.concatenate([q]*(bm//128),axis=1)
                        kv[u*UNIT+b:u*UNIT+b+cs,r:r+bm]=jnp.exp2(s+(q+sqr[0:1,r:r+bm])).astype(bf16)
                acc[:,r:r+bm]+=jnp.dot(pr,kv[u0*UNIT:(u0+ug)*UNIT,r:r+bm],preferred_element_type=f32)
        return 0

    lax.fori_loop(0,pairs,body,0)
    for j in range(nr): outs[j][...]=acc[:,j*ROWS:(j+1)*ROWS].astype(outs[j].dtype)


def rbf(off,rel,rows,pairs,init=None,out=f32,bm=256,cs=512,ug=4):
    nr=len(rows)
    args=list(rows)+[x for p in pairs for x in p]+([init] if init is not None else [])
    V = VM
    npairs=len(pairs); m=nr*ROWS
    return pl.pallas_call(functools.partial(rbf_kernel,nr=nr,pairs=npairs,with_init=init is not None,bm=bm,cs=cs,ug=ug),
        in_specs=[SM,V]+[V]*nr+[V]*(2*npairs)+([V] if init is not None else []),
        out_specs=[V]*nr,out_shape=[jax.ShapeDtypeStruct((64,ROWS),out)]*nr,
        scratch_shapes=[pltpu.VMEM((m,FEAT),bf16),pltpu.VMEM((8,m),f32),pltpu.VMEM((npairs*PAIR,FEAT),bf16),pltpu.VMEM((2048,128),f32),
          pltpu.VMEM((2048,m),bf16),pltpu.VMEM((64,m),f32),pltpu.SemaphoreType.DMA((2*npairs,))],
        compiler_params=LIMIT)(off,rel,*args)


def ring(shift):
    return [(i, (i + shift) % 4) for i in range(4)]


Z = ("zh", "zl")
SWAP = [(0, 1), (1, 0)]


def steps(x_m, dest, x_c, w1, b1, w2, b2, w3, rel, probes):
    rel = rel.reshape(1, FEAT)
    y = lax.axis_index("y").astype(jnp.int32)
    off = jnp.stack([y, (y + 3) % 4, (y + 1) % 4, (y + 2) % 4]).astype(jnp.int32)
    sent, own, probe = front(y.reshape(1), dest, x_m.T, x_c.T, probes.T, w1, b1, w2, b2, w3)
    u1 = lax.ppermute(own, "y", ring(1))
    u3 = lax.ppermute(own, "y", ring(3))
    u2 = lax.ppermute(own, "y", ring(2))
    got = lax.all_to_all(sent, ALL, 0, 0, tiled=True)
    u1, u3, u2, got = lax.optimization_barrier((u1, u3, u2, got))
    feats = row_net(got, w1, b1, w2, b2, w3)
    ca = jnp.concatenate([own, probe, u1[:256]], 0)
    cb = jnp.concatenate([u1[256:], u3, u2], 0)
    za = lax.ppermute(ca, Z, ring(1))
    zb = lax.ppermute(cb, Z, ring(3))
    pa = lax.ppermute(ca, "core", SWAP)
    pb = lax.ppermute(cb, "core", SWAP)
    f1 = lax.ppermute(feats, "x", ring(1))
    f3 = lax.ppermute(feats, "x", ring(3))
    za, zb, held = lax.optimization_barrier((za, zb, feats))
    pza = lax.ppermute(za, "core", SWAP)
    pzb = lax.ppermute(zb, "core", SWAP)
    near = [(ca, cb), (pa, pb)]
    far = [(za, zb), (pza, pzb)]
    (first,) = rbf(off, rel, [held], near, bm=512)
    f1, f3, first = lax.optimization_barrier((f1, f3, first))
    f2 = lax.ppermute(f1, "x", ring(1))
    t1, t3 = rbf(off, rel, [f1, f3], near + far, out=bf16)
    r1 = lax.ppermute(t1, "x", ring(3))
    r3 = lax.ppermute(t3, "x", ring(1))
    (t2,) = rbf(off, rel, [f2], near + far, out=bf16, bm=512)
    r2 = lax.ppermute(t2, "x", ring(2))
    (mine,) = rbf(off, rel, [held], far, first, bm=512)
    total = mine + r1.astype(f32) + r3.astype(f32) + r2.astype(f32)
    return total.T


def solution(mesh):
    fine = Mesh(mesh.devices.reshape(4, 2, 2, 4, 2), ALL)
    placed = (P(ALL, None), P(ALL), P(COL, None), P(), P(), P(), P(), P(), P(), P(COL, None))
    return jax.shard_map(steps, mesh=fine, in_specs=placed, out_specs=P(ALL, None), check_vma=False)
```

```python
import functools

import jax
import jax.numpy as jnp
from jax import lax
from jax.experimental import pallas as pl
from jax.experimental.pallas import tpu as pltpu
from jax.sharding import Mesh, PartitionSpec as P


f32 = jnp.float32
bf16 = jnp.bfloat16
NT = (((1,), (1,)), ((), ()))
TN = (((0,), (0,)), ((), ()))
ALL = ("y", "zh", "zl", "x", "core")
COL = ("zl", "x", "core")
LOG2E = 1.4426950408889634
ROWS = 512
FEAT = 256
UNIT = 512
PAIR = 2560


def dot(a, b):
    return jnp.dot(a, b, preferred_element_type=f32)


CHUNK = 512


def weight_copies(w2_ref, w3_ref, w2_v, w3_v, sem):
    chunks = w2_v.shape[0]
    for c in range(chunks):
        pltpu.make_async_copy(w2_ref.at[:, pl.ds(c * CHUNK, CHUNK)], w2_v.at[c], sem.at[c]).start()
        if c == 0:
            pltpu.make_async_copy(w3_ref, w3_v, sem.at[chunks]).start()


def last_layers(w2_ref, b2_ref, w3_ref, o_ref, h1, w2_v, w3_v, acc, sem):
    chunks = w2_v.shape[0]

    def chunk(c):
        pltpu.make_async_copy(w2_ref.at[:, pl.ds(0, CHUNK)], w2_v.at[c], sem.at[c]).wait()
        at = pl.multiple_of(c * CHUNK, CHUNK)
        h2 = jnp.maximum(dot(h1[...], w2_v[c]) + b2_ref[:, pl.ds(at, CHUNK)], 0.0).astype(bf16)
        return h2, at

    h2, _ = chunk(0)
    pltpu.make_async_copy(w3_ref, w3_v, sem.at[chunks]).wait()
    acc[...] = dot(h2, w3_v[0:CHUNK, :])

    def body(c, _):
        h2, at = chunk(c)
        acc[...] += dot(h2, w3_v[pl.ds(at, CHUNK), :])
        return 0

    lax.fori_loop(1, chunks, body, 0)
    o_ref[...] = acc[...].astype(bf16)


def reorder(dest_ref, xt_ref, o_ref):
    d_row = dest_ref[...]
    d_f = d_row.astype(f32)
    d_col = jnp.transpose(jnp.broadcast_to(d_f, (128, ROWS)))
    before = jnp.concatenate([d_col] * (ROWS // 128), axis=1) < d_f
    rank = jnp.sum(jnp.where(before, 1.0, 0.0), axis=0, keepdims=True)
    place = lax.broadcasted_iota(jnp.int32, (ROWS, ROWS), 0).astype(f32) == rank
    place = jnp.where(place, 1.0, 0.0).astype(bf16)
    pos = jnp.bitwise_and(d_row, ROWS - 1)
    high = jnp.right_shift(pos, 4).astype(f32)
    low = jnp.bitwise_and(pos, 15).astype(f32)
    line = lax.broadcasted_iota(jnp.int32, (88, ROWS), 0)
    extra = jnp.where(line == 0, high, jnp.where(line == 1, low, 0.0))
    ext = jnp.concatenate([xt_ref[...].astype(f32), extra], axis=0).astype(bf16)
    o_ref[...] = lax.dot_general(place, ext, NT, preferred_element_type=f32).astype(bf16)


def front_kernel(
    y_ref, dest_ref, xm_ref, xc_ref, p_ref, w1_ref, b1_ref, w2_ref, b2_ref, w3_ref,
    s_ref, o_ref, q_ref, h1, w2_v, w3_v, acc, sem,
):
    weight_copies(w2_ref, w3_ref, w2_v, w3_v, sem)
    reorder(dest_ref, xm_ref, s_ref)
    for j in range(8):
        q_ref[j * 64 : (j + 1) * 64, :] = p_ref[:, j * 256 : (j + 1) * 256].astype(bf16)
    xc = xc_ref[:, pl.ds(pl.multiple_of(y_ref[0] * UNIT, UNIT), UNIT)]
    x = lax.dot_general(xc, w1_ref[...], TN, preferred_element_type=f32)
    h1[...] = jnp.maximum(x + b1_ref[...], 0.0).astype(bf16)
    last_layers(w2_ref, b2_ref, w3_ref, o_ref, h1, w2_v, w3_v, acc, sem)


def row_kernel(r_ref, w1_ref, b1_ref, w2_ref, b2_ref, w3_ref, o_ref, h1, w2_v, w3_v, acc, sem):
    weight_copies(w2_ref, w3_ref, w2_v, w3_v, sem)
    got = r_ref[...]
    lane = lax.broadcasted_iota(jnp.int32, (8, 128), 1)
    pick = jnp.where(lane == 40, 16.0, jnp.where(lane == 41, 1.0, 0.0)).astype(bf16)
    pos = lax.dot_general(pick, got, NT, preferred_element_type=f32)[0:1, :]
    place = lax.broadcasted_iota(jnp.int32, (ROWS, ROWS), 0).astype(f32) == pos
    place = jnp.where(place, 1.0, 0.0).astype(bf16)
    x = dot(place, got).astype(bf16)[:, :40]
    h1[...] = jnp.maximum(dot(x, w1_ref[...]) + b1_ref[...], 0.0).astype(bf16)
    last_layers(w2_ref, b2_ref, w3_ref, o_ref, h1, w2_v, w3_v, acc, sem)


VM = pl.BlockSpec(memory_space=pltpu.VMEM)
SM = pl.BlockSpec(memory_space=pltpu.SMEM)
HB = pl.BlockSpec(memory_space=pltpu.HBM)
LIMIT = pltpu.CompilerParams(vmem_limit_bytes=22 * 2**20)
WEIGHT_SPECS = [VM, VM, HB, VM, HB]


def net_scratch(m, hid, ft):
    return [
        pltpu.VMEM((m, hid), bf16),
        pltpu.VMEM((hid // CHUNK, hid, CHUNK), bf16),
        pltpu.VMEM((hid, ft), bf16),
        pltpu.VMEM((m, ft), f32),
        pltpu.SemaphoreType.DMA((hid // CHUNK + 1,)),
    ]


def front(y, dest, x_m, x_c, p_t, w1, b1, w2, b2, w3):
    hid, ft = w2.shape[0], w3.shape[1]
    return pl.pallas_call(
        front_kernel,
        in_specs=[SM, VM, VM, VM, VM, *WEIGHT_SPECS],
        out_specs=[VM] * 3,
        out_shape=[
            jax.ShapeDtypeStruct((ROWS, 128), bf16),
            jax.ShapeDtypeStruct((UNIT, ft), bf16),
            jax.ShapeDtypeStruct((UNIT, ft), bf16),
        ],
        scratch_shapes=net_scratch(UNIT, hid, ft),
        name="front",
    )(y, dest.reshape(1, ROWS), x_m, x_c, p_t, w1, b1.reshape(1, -1), w2, b2.reshape(1, -1), w3)


def row_net(got, w1, b1, w2, b2, w3):
    hid, ft = w2.shape[0], w3.shape[1]
    return pl.pallas_call(
        row_kernel,
        in_specs=[VM, *WEIGHT_SPECS],
        out_specs=VM,
        out_shape=jax.ShapeDtypeStruct((ROWS, ft), bf16),
        scratch_shapes=net_scratch(ROWS, hid, ft),
        name="row_net",
    )(got, w1, b1.reshape(1, -1), w2, b2.reshape(1, -1), w3)


def rbf_kernel(off_ref,rel_ref,*refs,nr,pairs,with_init,bm,cs,ug):
    rows=refs[:nr]; refs=refs[nr:]
    cols=refs[:2*pairs]; refs=refs[2*pairs:]
    if with_init: init_ref,refs=refs[0],refs[1:]
    outs=refs[:nr]; refs=refs[nr:]
    sc,sqr,cv,sv,kv,acc,sem=refs
    m=nr*ROWS

    def copies(p,a,b):
        return (pltpu.make_async_copy(a,cv.at[pl.ds(pl.multiple_of(p*PAIR,PAIR),1280)],sem.at[2*p]),
                pltpu.make_async_copy(b,cv.at[pl.ds(pl.multiple_of(p*PAIR+1280,256),1280)],sem.at[2*p+1]))

    for p in range(pairs):
        for c in copies(p,cols[2*p],cols[2*p+1]): c.start()
    rel=rel_ref[...]
    ones=jnp.ones((8,FEAT),bf16)
    for j in range(nr):
        at=slice(j*ROWS,(j+1)*ROWS)
        rf=rows[j][...].astype(f32)
        sc[at,:]=(rf*(rel*LOG2E)).astype(bf16)
        w=rel*rf*rf
        hi=w.astype(bf16); lo=(w-hi.astype(f32)).astype(bf16)
        sqr[:,at]=(-0.5*LOG2E)*(lax.dot_general(ones,hi,NT,preferred_element_type=f32)+lax.dot_general(ones,lo,NT,preferred_element_type=f32))
        acc[:,at]=init_ref[...] if with_init else jnp.zeros((64,ROWS),f32)

    def body(p,_):
        for c in copies(p,cols[0],cols[1]): c.wait()
        starts=[pl.multiple_of(p*PAIR+(0 if u==0 else 512+u*512),512) for u in range(4)]
        for u0 in range(0,4,ug):
            us=range(u0,u0+ug)
            for u in us:
                c=cv[pl.ds(starts[u],UNIT),:].astype(f32)
                sv[u*UNIT:(u+1)*UNIT,:]=jnp.broadcast_to((-0.5*LOG2E)*jnp.sum(rel*c*c,axis=1,keepdims=True),(UNIT,128))
            prs=[]
            for u in us:
                st=pl.multiple_of(p*PAIR+512+off_ref[u]*128,128)
                prs+=[cv[pl.ds(st,64),:],cv[pl.ds(st+64,64),:]]
            pr=jnp.concatenate(prs,axis=1)
            for r in range(0,m,bm):
                for u in us:
                    for b in range(0,UNIT,cs):
                        s=lax.dot_general(cv[pl.ds(starts[u]+b,cs),:],sc[r:r+bm,:],NT,preferred_element_type=f32)
                        q=sv[u*UNIT+b:u*UNIT+b+cs,:]
                        q=jnp.concatenate([q]*(bm//128),axis=1)
                        kv[u*UNIT+b:u*UNIT+b+cs,r:r+bm]=jnp.exp2(s+(q+sqr[0:1,r:r+bm])).astype(bf16)
                acc[:,r:r+bm]+=jnp.dot(pr,kv[u0*UNIT:(u0+ug)*UNIT,r:r+bm],preferred_element_type=f32)
        return 0

    lax.fori_loop(0,pairs,body,0)
    for j in range(nr): outs[j][...]=acc[:,j*ROWS:(j+1)*ROWS].astype(outs[j].dtype)


def rbf(off,rel,rows,pairs,init=None,out=f32,bm=256,cs=512,ug=4):
    nr=len(rows)
    args=list(rows)+[x for p in pairs for x in p]+([init] if init is not None else [])
    V = VM
    npairs=len(pairs); m=nr*ROWS
    return pl.pallas_call(functools.partial(rbf_kernel,nr=nr,pairs=npairs,with_init=init is not None,bm=bm,cs=cs,ug=ug),
        in_specs=[SM,V]+[V]*nr+[V]*(2*npairs)+([V] if init is not None else []),
        out_specs=[V]*nr,out_shape=[jax.ShapeDtypeStruct((64,ROWS),out)]*nr,
        scratch_shapes=[pltpu.VMEM((m,FEAT),bf16),pltpu.VMEM((8,m),f32),pltpu.VMEM((npairs*PAIR,FEAT),bf16),pltpu.VMEM((2048,128),f32),
          pltpu.VMEM((2048,m),bf16),pltpu.VMEM((64,m),f32),pltpu.SemaphoreType.DMA((2*npairs,))],
        compiler_params=LIMIT)(off,rel,*args)


def ring(shift):
    return [(i, (i + shift) % 4) for i in range(4)]


Z = ("zh", "zl")
SWAP = [(0, 1), (1, 0)]


def steps(x_m, dest, x_c, w1, b1, w2, b2, w3, rel, probes):
    rel = rel.reshape(1, FEAT)
    y = lax.axis_index("y").astype(jnp.int32)
    off = jnp.stack([y, (y + 3) % 4, (y + 1) % 4, (y + 2) % 4]).astype(jnp.int32)
    sent, own, probe = front(y.reshape(1), dest, x_m.T, x_c.T, probes.T, w1, b1, w2, b2, w3)
    u1 = lax.ppermute(own, "y", ring(1))
    u3 = lax.ppermute(own, "y", ring(3))
    u2 = lax.ppermute(own, "y", ring(2))
    got = lax.all_to_all(sent, ALL, 0, 0, tiled=True)
    u1, u3, u2, got = lax.optimization_barrier((u1, u3, u2, got))
    feats = row_net(got, w1, b1, w2, b2, w3)
    ca = jnp.concatenate([own, probe, u1[:256]], 0)
    cb = jnp.concatenate([u1[256:], u3, u2], 0)
    za = lax.ppermute(ca, Z, ring(1))
    zb = lax.ppermute(cb, Z, ring(3))
    pa = lax.ppermute(ca, "core", SWAP)
    pb = lax.ppermute(cb, "core", SWAP)
    f1 = lax.ppermute(feats, "x", ring(1))
    f3 = lax.ppermute(feats, "x", ring(3))
    held = pltpu.with_memory_space_constraint(feats, pltpu.HBM)
    near = [(ca, cb), (pa, pb)]
    (first,) = rbf(off, rel, [held], near[:1], bm=512)
    za, zb, first = lax.optimization_barrier((za, zb, first))
    pza = lax.ppermute(za, "core", SWAP)
    pzb = lax.ppermute(zb, "core", SWAP)
    far = [(za, zb), (pza, pzb)]
    (first,) = rbf(off, rel, [held], near[1:], first, bm=512)
    f1, f3, first = lax.optimization_barrier((f1, f3, first))
    f2 = lax.ppermute(f1, "x", ring(1))
    t1, t3 = rbf(off, rel, [f1, f3], near + far, out=bf16)
    r1 = lax.ppermute(t1, "x", ring(3))
    r3 = lax.ppermute(t3, "x", ring(1))
    (t2,) = rbf(off, rel, [f2], near + far, out=bf16, bm=512)
    r2 = lax.ppermute(t2, "x", ring(2))
    (mine,) = rbf(off, rel, [held], far, first, bm=512)
    total = mine + r1.astype(f32) + r3.astype(f32) + r2.astype(f32)
    return total.T


def solution(mesh):
    fine = Mesh(mesh.devices.reshape(4, 2, 2, 4, 2), ALL)
    placed = (P(ALL, None), P(ALL), P(COL, None), P(), P(), P(), P(), P(), P(), P(COL, None))
    return jax.shard_map(steps, mesh=fine, in_specs=placed, out_specs=P(ALL, None), check_vma=False)
```

```python
import functools

import jax
import jax.numpy as jnp
from jax import lax
from jax.experimental import pallas as pl
from jax.experimental.pallas import tpu as pltpu
from jax.sharding import Mesh, PartitionSpec as P


f32 = jnp.float32
bf16 = jnp.bfloat16
NT = (((1,), (1,)), ((), ()))
TN = (((0,), (0,)), ((), ()))
ALL = ("y", "zh", "zl", "x", "core")
COL = ("zl", "x", "core")
LOG2E = 1.4426950408889634
ROWS = 512
FEAT = 256
UNIT = 512


def dot(a, b):
    return jnp.dot(a, b, preferred_element_type=f32)


CHUNK = 512


def weight_copies(w2_ref, w3_ref, w2_v, w3_v, sem):
    chunks = w2_v.shape[0]
    for c in range(chunks):
        pltpu.make_async_copy(w2_ref.at[:, pl.ds(c * CHUNK, CHUNK)], w2_v.at[c], sem.at[c]).start()
        if c == 0:
            pltpu.make_async_copy(w3_ref, w3_v, sem.at[chunks]).start()


def last_layers(w2_ref, b2_ref, w3_ref, o_ref, h1, w2_v, w3_v, acc, sem):
    chunks = w2_v.shape[0]

    def chunk(c):
        pltpu.make_async_copy(w2_ref.at[:, pl.ds(0, CHUNK)], w2_v.at[c], sem.at[c]).wait()
        at = pl.multiple_of(c * CHUNK, CHUNK)
        h2 = jnp.maximum(dot(h1[...], w2_v[c]) + b2_ref[:, pl.ds(at, CHUNK)], 0.0).astype(bf16)
        return h2, at

    h2, _ = chunk(0)
    pltpu.make_async_copy(w3_ref, w3_v, sem.at[chunks]).wait()
    acc[...] = dot(h2, w3_v[0:CHUNK, :])

    def body(c, _):
        h2, at = chunk(c)
        acc[...] += dot(h2, w3_v[pl.ds(at, CHUNK), :])
        return 0

    lax.fori_loop(1, chunks, body, 0)
    o_ref[...] = acc[...].astype(bf16)


def reorder(dest_ref, xt_ref, o_ref):
    d_row = dest_ref[...]
    d_f = d_row.astype(f32)
    d_col = jnp.transpose(jnp.broadcast_to(d_f, (128, ROWS)))
    before = jnp.concatenate([d_col] * (ROWS // 128), axis=1) < d_f
    rank = jnp.sum(jnp.where(before, 1.0, 0.0), axis=0, keepdims=True)
    place = lax.broadcasted_iota(jnp.int32, (ROWS, ROWS), 0).astype(f32) == rank
    place = jnp.where(place, 1.0, 0.0).astype(bf16)
    pos = jnp.bitwise_and(d_row, ROWS - 1)
    high = jnp.right_shift(pos, 4).astype(f32)
    low = jnp.bitwise_and(pos, 15).astype(f32)
    line = lax.broadcasted_iota(jnp.int32, (88, ROWS), 0)
    extra = jnp.where(line == 0, high, jnp.where(line == 1, low, 0.0))
    ext = jnp.concatenate([xt_ref[...].astype(f32), extra], axis=0).astype(bf16)
    o_ref[...] = lax.dot_general(place, ext, NT, preferred_element_type=f32).astype(bf16)


def front_kernel(
    y_ref, dest_ref, xm_ref, xc_ref, p_ref, w1_ref, b1_ref, w2_ref, b2_ref, w3_ref,
    s_ref, o_ref, q_ref, h1, w2_v, w3_v, acc, sem,
):
    weight_copies(w2_ref, w3_ref, w2_v, w3_v, sem)
    reorder(dest_ref, xm_ref, s_ref)
    for j in range(8):
        q_ref[j * 64 : (j + 1) * 64, :] = p_ref[:, j * 256 : (j + 1) * 256].astype(bf16)
    xc = xc_ref[:, pl.ds(pl.multiple_of(y_ref[0] * UNIT, UNIT), UNIT)]
    x = lax.dot_general(xc, w1_ref[...], TN, preferred_element_type=f32)
    h1[...] = jnp.maximum(x + b1_ref[...], 0.0).astype(bf16)
    last_layers(w2_ref, b2_ref, w3_ref, o_ref, h1, w2_v, w3_v, acc, sem)


def row_kernel(r_ref, w1_ref, b1_ref, w2_ref, b2_ref, w3_ref, o_ref, h1, w2_v, w3_v, acc, sem):
    weight_copies(w2_ref, w3_ref, w2_v, w3_v, sem)
    got = r_ref[...]
    lane = lax.broadcasted_iota(jnp.int32, (8, 128), 1)
    pick = jnp.where(lane == 40, 16.0, jnp.where(lane == 41, 1.0, 0.0)).astype(bf16)
    pos = lax.dot_general(pick, got, NT, preferred_element_type=f32)[0:1, :]
    place = lax.broadcasted_iota(jnp.int32, (ROWS, ROWS), 0).astype(f32) == pos
    place = jnp.where(place, 1.0, 0.0).astype(bf16)
    x = dot(place, got).astype(bf16)[:, :40]
    h1[...] = jnp.maximum(dot(x, w1_ref[...]) + b1_ref[...], 0.0).astype(bf16)
    last_layers(w2_ref, b2_ref, w3_ref, o_ref, h1, w2_v, w3_v, acc, sem)


VM = pl.BlockSpec(memory_space=pltpu.VMEM)
SM = pl.BlockSpec(memory_space=pltpu.SMEM)
HB = pl.BlockSpec(memory_space=pltpu.HBM)
LIMIT = pltpu.CompilerParams(vmem_limit_bytes=22 * 2**20)
WEIGHT_SPECS = [VM, VM, HB, VM, HB]


def net_scratch(m, hid, ft):
    return [
        pltpu.VMEM((m, hid), bf16),
        pltpu.VMEM((hid // CHUNK, hid, CHUNK), bf16),
        pltpu.VMEM((hid, ft), bf16),
        pltpu.VMEM((m, ft), f32),
        pltpu.SemaphoreType.DMA((hid // CHUNK + 1,)),
    ]


def front(y, dest, x_m, x_c, p_t, w1, b1, w2, b2, w3):
    hid, ft = w2.shape[0], w3.shape[1]
    return pl.pallas_call(
        front_kernel,
        in_specs=[SM, VM, VM, VM, VM, *WEIGHT_SPECS],
        out_specs=[VM] * 3,
        out_shape=[
            jax.ShapeDtypeStruct((ROWS, 128), bf16),
            jax.ShapeDtypeStruct((UNIT, ft), bf16),
            jax.ShapeDtypeStruct((UNIT, ft), bf16),
        ],
        scratch_shapes=net_scratch(UNIT, hid, ft),
        name="front",
    )(y, dest.reshape(1, ROWS), x_m, x_c, p_t, w1, b1.reshape(1, -1), w2, b2.reshape(1, -1), w3)


def row_net(got, w1, b1, w2, b2, w3):
    hid, ft = w2.shape[0], w3.shape[1]
    return pl.pallas_call(
        row_kernel,
        in_specs=[VM, *WEIGHT_SPECS],
        out_specs=VM,
        out_shape=jax.ShapeDtypeStruct((ROWS, ft), bf16),
        scratch_shapes=net_scratch(ROWS, hid, ft),
        compiler_params=pltpu.CompilerParams(vmem_limit_bytes=57 * 2**20),
        name="row_net",
    )(got, w1, b1.reshape(1, -1), w2, b2.reshape(1, -1), w3)


def rbf_kernel(off_ref, rel_ref, *refs, nr, pairs, with_init, bm):
    rows, refs = refs[:nr], refs[nr:]
    cols, refs = refs[: 2 * pairs], refs[2 * pairs :]
    if with_init:
        init_ref, refs = refs[0], refs[1:]
    outs, refs = refs[:nr], refs[nr:]
    sc, sqr, sv, kv, acc = refs
    m = nr * ROWS
    rel = rel_ref[...]
    ones = jnp.ones((8, FEAT), bf16)
    for j in range(nr):
        at = slice(j * ROWS, (j + 1) * ROWS)
        rf = rows[j][...].astype(f32)
        sc[at, :] = (rf * (rel * LOG2E)).astype(bf16)
        w = rel * rf * rf
        hi = w.astype(bf16)
        lo = (w - hi.astype(f32)).astype(bf16)
        sqr[:, at] = (-0.5 * LOG2E) * (
            lax.dot_general(ones, hi, NT, preferred_element_type=f32)
            + lax.dot_general(ones, lo, NT, preferred_element_type=f32)
        )
        acc[:, at] = init_ref[...] if with_init else jnp.zeros((64, ROWS), f32)
    for p in range(pairs):
        a_ref, b_ref = cols[2 * p], cols[2 * p + 1]
        blocks = ((a_ref, 0, 512), (a_ref, 1024, 256), (b_ref, 0, 256), (b_ref, 256, 512), (b_ref, 768, 512))
        slot = p % 2
        to = 0
        for ref, at, size in blocks:
            c = ref[at : at + size, :].astype(f32)
            total = jnp.sum(rel * c * c, axis=1, keepdims=True)
            sv[slot, to : to + size, :] = jnp.broadcast_to((-0.5 * LOG2E) * total, (size, 128))
            to += size
        probe = []
        for u in range(4):
            at = pl.multiple_of(512 + off_ref[u] * 128, 128)
            probe += [a_ref[pl.ds(at, 64), :], a_ref[pl.ds(at + 64, 64), :]]
        probe = jnp.concatenate(probe, axis=1)
        for r in range(0, m, bm):
            to = 0
            for ref, at, size in blocks:
                s = lax.dot_general(ref[at : at + size, :], sc[r : r + bm, :], NT, preferred_element_type=f32)
                q = jnp.concatenate([sv[slot, to : to + size, :]] * (bm // 128), axis=1)
                kv[slot, to : to + size, r : r + bm] = jnp.exp2(s + (q + sqr[0:1, r : r + bm])).astype(bf16)
                to += size
            acc[:, r : r + bm] += dot(probe, kv[slot, :, r : r + bm])
    for j in range(nr):
        outs[j][...] = acc[:, j * ROWS : (j + 1) * ROWS].astype(outs[j].dtype)


def rbf(off, rel, rows, col_pairs, init=None, out=f32, bm=256):
    nr, pairs = len(rows), len(col_pairs)
    args = [*rows, *(x for pair in col_pairs for x in pair), *([] if init is None else [init])]
    m = nr * ROWS
    return pl.pallas_call(
        functools.partial(rbf_kernel, nr=nr, pairs=pairs, with_init=init is not None, bm=bm),
        in_specs=[SM, VM] + [VM] * len(args),
        out_specs=[VM] * nr,
        out_shape=[jax.ShapeDtypeStruct((64, ROWS), out)] * nr,
        scratch_shapes=[
            pltpu.VMEM((m, FEAT), bf16),
            pltpu.VMEM((8, m), f32),
            pltpu.VMEM((2, 2048, 128), f32),
            pltpu.VMEM((2, 2048, m), bf16),
            pltpu.VMEM((64, m), f32),
        ],
        compiler_params=LIMIT,
    )(off, rel, *args)


def ring(shift):
    return [(i, (i + shift) % 4) for i in range(4)]


Z = ("zh", "zl")
SWAP = [(0, 1), (1, 0)]


def steps(x_m, dest, x_c, w1, b1, w2, b2, w3, rel, probes):
    rel = rel.reshape(1, FEAT)
    y = lax.axis_index("y").astype(jnp.int32)
    off = jnp.stack([y, (y + 3) % 4, (y + 1) % 4, (y + 2) % 4]).astype(jnp.int32)
    sent, own, probe = front(y.reshape(1), dest, x_m.T, x_c.T, probes.T, w1, b1, w2, b2, w3)
    u1 = lax.ppermute(own, "y", ring(1))
    u3 = lax.ppermute(own, "y", ring(3))
    u2 = lax.ppermute(own, "y", ring(2))
    got = lax.all_to_all(sent, ALL, 0, 0, tiled=True)
    u1, u3, u2, got = lax.optimization_barrier((u1, u3, u2, got))
    feats = row_net(got, w1, b1, w2, b2, w3)
    ca = jnp.concatenate([own, probe, u1[:256]], 0)
    cb = jnp.concatenate([u1[256:], u3, u2], 0)
    za = lax.ppermute(ca, Z, ring(1))
    zb = lax.ppermute(cb, Z, ring(3))
    pa = lax.ppermute(ca, "core", SWAP)
    pb = lax.ppermute(cb, "core", SWAP)
    f1 = lax.ppermute(feats, "x", ring(1))
    f3 = lax.ppermute(feats, "x", ring(3))
    held = pltpu.with_memory_space_constraint(feats, pltpu.VMEM)
    near = [(ca, cb), (pa, pb)]
    (first,) = rbf(off, rel, [held], near[:1], bm=512)
    za, zb, first = lax.optimization_barrier((za, zb, first))
    pza = lax.ppermute(za, "core", SWAP)
    pzb = lax.ppermute(zb, "core", SWAP)
    far = [(za, zb), (pza, pzb)]
    (first,) = rbf(off, rel, [held], near[1:], first, bm=512)
    f1, f3, first = lax.optimization_barrier((f1, f3, first))
    f2 = lax.ppermute(f1, "x", ring(1))
    t1, t3 = rbf(off, rel, [f1, f3], near + far, out=bf16)
    r1 = lax.ppermute(t1, "x", ring(3))
    r3 = lax.ppermute(t3, "x", ring(1))
    (t2,) = rbf(off, rel, [f2], near + far, out=bf16, bm=512)
    r2 = lax.ppermute(t2, "x", ring(2))
    (mine,) = rbf(off, rel, [held], far, first, bm=512)
    total = mine + r1.astype(f32) + r3.astype(f32) + r2.astype(f32)
    return total.T


def solution(mesh):
    fine = Mesh(mesh.devices.reshape(4, 2, 2, 4, 2), ALL)
    placed = (P(ALL, None), P(ALL), P(COL, None), P(), P(), P(), P(), P(), P(), P(COL, None))
    return jax.shard_map(steps, mesh=fine, in_specs=placed, out_specs=P(ALL, None), check_vma=False)
```

```python
import functools

import jax
import jax.numpy as jnp
from jax import lax
from jax.experimental import pallas as pl
from jax.experimental.pallas import tpu as pltpu
from jax.sharding import Mesh, PartitionSpec as P


f32 = jnp.float32
bf16 = jnp.bfloat16
NT = (((1,), (1,)), ((), ()))
TN = (((0,), (0,)), ((), ()))
ALL = ("y", "zh", "zl", "x", "core")
COL = ("zl", "x", "core")
LOG2E = 1.4426950408889634
ROWS = 512
FEAT = 256
UNIT = 512


def dot(a, b):
    return jnp.dot(a, b, preferred_element_type=f32)


CHUNK = 512


def weight_copies(w2_ref, w3_ref, w2_v, w3_v, sem):
    chunks = w2_v.shape[0]
    for c in range(chunks):
        pltpu.make_async_copy(w2_ref.at[:, pl.ds(c * CHUNK, CHUNK)], w2_v.at[c], sem.at[c]).start()
        if c == 0:
            pltpu.make_async_copy(w3_ref, w3_v, sem.at[chunks]).start()


def last_layers(w2_ref, b2_ref, w3_ref, o_ref, h1, w2_v, w3_v, acc, sem):
    chunks = w2_v.shape[0]

    def chunk(c):
        pltpu.make_async_copy(w2_ref.at[:, pl.ds(0, CHUNK)], w2_v.at[c], sem.at[c]).wait()
        at = pl.multiple_of(c * CHUNK, CHUNK)
        h2 = jnp.maximum(dot(h1[...], w2_v[c]) + b2_ref[:, pl.ds(at, CHUNK)], 0.0).astype(bf16)
        return h2, at

    h2, _ = chunk(0)
    pltpu.make_async_copy(w3_ref, w3_v, sem.at[chunks]).wait()
    acc[...] = dot(h2, w3_v[0:CHUNK, :])

    def body(c, _):
        h2, at = chunk(c)
        acc[...] += dot(h2, w3_v[pl.ds(at, CHUNK), :])
        return 0

    lax.fori_loop(1, chunks, body, 0)
    o_ref[...] = acc[...].astype(bf16)


def reorder(dest_ref, xt_ref, o_ref):
    d_row = dest_ref[...]
    d_f = d_row.astype(f32)
    d_col = jnp.transpose(jnp.broadcast_to(d_f, (128, ROWS)))
    before = jnp.concatenate([d_col] * (ROWS // 128), axis=1) < d_f
    rank = jnp.sum(jnp.where(before, 1.0, 0.0), axis=0, keepdims=True)
    place = lax.broadcasted_iota(jnp.int32, (ROWS, ROWS), 0).astype(f32) == rank
    place = jnp.where(place, 1.0, 0.0).astype(bf16)
    pos = jnp.bitwise_and(d_row, ROWS - 1)
    high = jnp.right_shift(pos, 4).astype(f32)
    low = jnp.bitwise_and(pos, 15).astype(f32)
    line = lax.broadcasted_iota(jnp.int32, (88, ROWS), 0)
    extra = jnp.where(line == 0, high, jnp.where(line == 1, low, 0.0))
    ext = jnp.concatenate([xt_ref[...].astype(f32), extra], axis=0).astype(bf16)
    o_ref[...] = lax.dot_general(place, ext, NT, preferred_element_type=f32).astype(bf16)


def front_kernel(
    y_ref, dest_ref, xm_ref, xc_ref, p_ref, w1_ref, b1_ref, w2_ref, b2_ref, w3_ref,
    s_ref, o_ref, q_ref, h1, w2_v, w3_v, acc, sem,
):
    weight_copies(w2_ref, w3_ref, w2_v, w3_v, sem)
    reorder(dest_ref, xm_ref, s_ref)
    for j in range(8):
        q_ref[j * 64 : (j + 1) * 64, :] = p_ref[:, j * 256 : (j + 1) * 256].astype(bf16)
    xc = xc_ref[:, pl.ds(pl.multiple_of(y_ref[0] * UNIT, UNIT), UNIT)]
    x = lax.dot_general(xc, w1_ref[...], TN, preferred_element_type=f32)
    h1[...] = jnp.maximum(x + b1_ref[...], 0.0).astype(bf16)
    last_layers(w2_ref, b2_ref, w3_ref, o_ref, h1, w2_v, w3_v, acc, sem)


def row_kernel(r_ref, w1_ref, b1_ref, w2_ref, b2_ref, w3_ref, o_ref, h1, w2_v, w3_v, acc, sem):
    weight_copies(w2_ref, w3_ref, w2_v, w3_v, sem)
    got = r_ref[...]
    lane = lax.broadcasted_iota(jnp.int32, (8, 128), 1)
    pick = jnp.where(lane == 40, 16.0, jnp.where(lane == 41, 1.0, 0.0)).astype(bf16)
    pos = lax.dot_general(pick, got, NT, preferred_element_type=f32)[0:1, :]
    place = lax.broadcasted_iota(jnp.int32, (ROWS, ROWS), 0).astype(f32) == pos
    place = jnp.where(place, 1.0, 0.0).astype(bf16)
    x = dot(place, got).astype(bf16)[:, :40]
    h1[...] = jnp.maximum(dot(x, w1_ref[...]) + b1_ref[...], 0.0).astype(bf16)
    last_layers(w2_ref, b2_ref, w3_ref, o_ref, h1, w2_v, w3_v, acc, sem)


VM = pl.BlockSpec(memory_space=pltpu.VMEM)
SM = pl.BlockSpec(memory_space=pltpu.SMEM)
HB = pl.BlockSpec(memory_space=pltpu.HBM)
LIMIT = pltpu.CompilerParams(vmem_limit_bytes=22 * 2**20)
WEIGHT_SPECS = [VM, VM, HB, VM, HB]


def net_scratch(m, hid, ft):
    return [
        pltpu.VMEM((m, hid), bf16),
        pltpu.VMEM((hid // CHUNK, hid, CHUNK), bf16),
        pltpu.VMEM((hid, ft), bf16),
        pltpu.VMEM((m, ft), f32),
        pltpu.SemaphoreType.DMA((hid // CHUNK + 1,)),
    ]


def front(y, dest, x_m, x_c, p_t, w1, b1, w2, b2, w3):
    hid, ft = w2.shape[0], w3.shape[1]
    return pl.pallas_call(
        front_kernel,
        in_specs=[SM, VM, VM, VM, VM, *WEIGHT_SPECS],
        out_specs=[VM] * 3,
        out_shape=[
            jax.ShapeDtypeStruct((ROWS, 128), bf16),
            jax.ShapeDtypeStruct((UNIT, ft), bf16),
            jax.ShapeDtypeStruct((UNIT, ft), bf16),
        ],
        scratch_shapes=net_scratch(UNIT, hid, ft),
        name="front",
    )(y, dest.reshape(1, ROWS), x_m, x_c, p_t, w1, b1.reshape(1, -1), w2, b2.reshape(1, -1), w3)


def row_net(got, w1, b1, w2, b2, w3):
    hid, ft = w2.shape[0], w3.shape[1]
    return pl.pallas_call(
        row_kernel,
        in_specs=[VM, *WEIGHT_SPECS],
        out_specs=VM,
        out_shape=jax.ShapeDtypeStruct((ROWS, ft), bf16),
        scratch_shapes=net_scratch(ROWS, hid, ft),
        compiler_params=pltpu.CompilerParams(vmem_limit_bytes=57 * 2**20),
        name="row_net",
    )(got, w1, b1.reshape(1, -1), w2, b2.reshape(1, -1), w3)


def rbf_kernel(off_ref, rel_ref, *refs, nr, pairs, with_init, bm):
    rows, refs = refs[:nr], refs[nr:]
    cols, refs = refs[: 2 * pairs], refs[2 * pairs :]
    if with_init:
        init_ref, refs = refs[0], refs[1:]
    outs, refs = refs[:nr], refs[nr:]
    sc, sqr, sv, kv, acc = refs
    m = nr * ROWS
    rel = rel_ref[...]
    ones = jnp.ones((8, FEAT), bf16)
    for j in range(nr):
        at = slice(j * ROWS, (j + 1) * ROWS)
        rf = rows[j][...].astype(f32)
        sc[at, :] = (rf * (rel * LOG2E)).astype(bf16)
        w = rel * rf * rf
        hi = w.astype(bf16)
        lo = (w - hi.astype(f32)).astype(bf16)
        sqr[:, at] = (-0.5 * LOG2E) * (
            lax.dot_general(ones, hi, NT, preferred_element_type=f32)
            + lax.dot_general(ones, lo, NT, preferred_element_type=f32)
        )
        acc[:, at] = init_ref[...] if with_init else jnp.zeros((64, ROWS), f32)
    for p in range(pairs):
        a_ref, b_ref = cols[2 * p], cols[2 * p + 1]
        blocks = ((a_ref, 0, 512), (a_ref, 1024, 256), (b_ref, 0, 256), (b_ref, 256, 512), (b_ref, 768, 512))
        slot = p % 2
        to = 0
        for ref, at, size in blocks:
            c = ref[at : at + size, :].astype(f32)
            total = jnp.sum(rel * c * c, axis=1, keepdims=True)
            sv[slot, to : to + size, :] = jnp.broadcast_to((-0.5 * LOG2E) * total, (size, 128))
            to += size
        probe = []
        for u in range(4):
            at = pl.multiple_of(512 + off_ref[u] * 128, 128)
            probe += [a_ref[pl.ds(at, 64), :], a_ref[pl.ds(at + 64, 64), :]]
        probe = jnp.concatenate(probe, axis=1)
        for r in range(0, m, bm):
            to = 0
            for ref, at, size in blocks:
                s = lax.dot_general(ref[at : at + size, :], sc[r : r + bm, :], NT, preferred_element_type=f32)
                q = jnp.concatenate([sv[slot, to : to + size, :]] * (bm // 128), axis=1)
                kv[slot, to : to + size, r : r + bm] = jnp.exp2(s + (q + sqr[0:1, r : r + bm])).astype(bf16)
                to += size
            acc[:, r : r + bm] += dot(probe, kv[slot, :, r : r + bm])
    for j in range(nr):
        outs[j][...] = acc[:, j * ROWS : (j + 1) * ROWS].astype(outs[j].dtype)


def rbf(off, rel, rows, col_pairs, init=None, out=f32, bm=256):
    nr, pairs = len(rows), len(col_pairs)
    args = [*rows, *(x for pair in col_pairs for x in pair), *([] if init is None else [init])]
    m = nr * ROWS
    return pl.pallas_call(
        functools.partial(rbf_kernel, nr=nr, pairs=pairs, with_init=init is not None, bm=bm),
        in_specs=[SM, VM] + [VM] * len(args),
        out_specs=[VM] * nr,
        out_shape=[jax.ShapeDtypeStruct((64, ROWS), out)] * nr,
        scratch_shapes=[
            pltpu.VMEM((m, FEAT), bf16),
            pltpu.VMEM((8, m), f32),
            pltpu.VMEM((2, 2048, 128), f32),
            pltpu.VMEM((2, 2048, m), bf16),
            pltpu.VMEM((64, m), f32),
        ],
        compiler_params=LIMIT,
    )(off, rel, *args)


def ring(shift):
    return [(i, (i + shift) % 4) for i in range(4)]


Z = ("zh", "zl")
SWAP = [(0, 1), (1, 0)]


def steps(x_m, dest, x_c, w1, b1, w2, b2, w3, rel, probes):
    rel = rel.reshape(1, FEAT)
    y = lax.axis_index("y").astype(jnp.int32)
    off = jnp.stack([y, (y + 3) % 4, (y + 1) % 4, (y + 2) % 4]).astype(jnp.int32)
    sent, own, probe = front(y.reshape(1), dest, x_m.T, x_c.T, probes.T, w1, b1, w2, b2, w3)
    u1 = lax.ppermute(own, "y", ring(1))
    u3 = lax.ppermute(own, "y", ring(3))
    u2 = lax.ppermute(own, "y", ring(2))
    got = lax.all_to_all(sent, ALL, 0, 0, tiled=True)
    u1, u3, u2, got = lax.optimization_barrier((u1, u3, u2, got))
    feats = row_net(got, w1, b1, w2, b2, w3)
    ca = jnp.concatenate([own, probe, u1[:256]], 0)
    cb = jnp.concatenate([u1[256:], u3, u2], 0)
    za = lax.ppermute(ca, Z, ring(1))
    zb = lax.ppermute(cb, Z, ring(3))
    pa = lax.ppermute(ca, "core", SWAP)
    pb = lax.ppermute(cb, "core", SWAP)
    f1 = lax.ppermute(feats, "x", ring(1))
    f3 = lax.ppermute(feats, "x", ring(3))
    near = [(ca, cb), (pa, pb)]
    held = pltpu.with_memory_space_constraint(feats, pltpu.HBM)
    (first,) = rbf(off, rel, [held], near[:1])
    za, zb, first = lax.optimization_barrier((za, zb, first))
    pza = lax.ppermute(za, "core", SWAP)
    pzb = lax.ppermute(zb, "core", SWAP)
    far = [(za, zb), (pza, pzb)]
    (first,) = rbf(off, rel, [feats], near[1:], first)
    f1, f3, first = lax.optimization_barrier((f1, f3, first))
    f2 = lax.ppermute(f1, "x", ring(1))
    t1, t3 = rbf(off, rel, [f1, f3], near + far, out=bf16)
    r1 = lax.ppermute(t1, "x", ring(3))
    r3 = lax.ppermute(t3, "x", ring(1))
    (t2,) = rbf(off, rel, [f2], near + far, out=bf16)
    r2 = lax.ppermute(t2, "x", ring(2))
    (mine,) = rbf(off, rel, [feats], far, first)
    total = mine + r1.astype(f32) + r3.astype(f32) + r2.astype(f32)
    return total.T


def solution(mesh):
    fine = Mesh(mesh.devices.reshape(4, 2, 2, 4, 2), ALL)
    placed = (P(ALL, None), P(ALL), P(COL, None), P(), P(), P(), P(), P(), P(), P(COL, None))
    return jax.shard_map(steps, mesh=fine, in_specs=placed, out_specs=P(ALL, None), check_vma=False)
```

```python
import functools

import jax
import jax.numpy as jnp
from jax import lax
from jax.experimental import pallas as pl
from jax.experimental.pallas import tpu as pltpu
from jax.sharding import Mesh, PartitionSpec as P


f32 = jnp.float32
bf16 = jnp.bfloat16
NT = (((1,), (1,)), ((), ()))
TN = (((0,), (0,)), ((), ()))
ALL = ("y", "zh", "zl", "x", "core")
COL = ("zl", "x", "core")
LOG2E = 1.4426950408889634
ROWS = 512
FEAT = 256
UNIT = 512


def dot(a, b):
    return jnp.dot(a, b, preferred_element_type=f32)


CHUNK = 512


def weight_copies(w2_ref, w3_ref, w2_v, w3_v, sem):
    chunks = w2_v.shape[0]
    for c in range(chunks):
        pltpu.make_async_copy(w2_ref.at[:, pl.ds(c * CHUNK, CHUNK)], w2_v.at[c], sem.at[c]).start()
        if c == 0:
            pltpu.make_async_copy(w3_ref, w3_v, sem.at[chunks]).start()


def last_layers(w2_ref, b2_ref, w3_ref, o_ref, h1, w2_v, w3_v, acc, sem):
    chunks = w2_v.shape[0]

    def chunk(c):
        pltpu.make_async_copy(w2_ref.at[:, pl.ds(0, CHUNK)], w2_v.at[c], sem.at[c]).wait()
        at = pl.multiple_of(c * CHUNK, CHUNK)
        h2 = jnp.maximum(dot(h1[...], w2_v[c]) + b2_ref[:, pl.ds(at, CHUNK)], 0.0).astype(bf16)
        return h2, at

    h2, _ = chunk(0)
    pltpu.make_async_copy(w3_ref, w3_v, sem.at[chunks]).wait()
    acc[...] = dot(h2, w3_v[0:CHUNK, :])

    def body(c, _):
        h2, at = chunk(c)
        acc[...] += dot(h2, w3_v[pl.ds(at, CHUNK), :])
        return 0

    lax.fori_loop(1, chunks, body, 0)
    o_ref[...] = acc[...].astype(bf16)


def reorder(dest_ref, xt_ref, o_ref):
    d_row = dest_ref[...]
    d_f = d_row.astype(f32)
    d_col = jnp.transpose(jnp.broadcast_to(d_f, (128, ROWS)))
    before = jnp.concatenate([d_col] * (ROWS // 128), axis=1) < d_f
    rank = jnp.sum(jnp.where(before, 1.0, 0.0), axis=0, keepdims=True)
    place = lax.broadcasted_iota(jnp.int32, (ROWS, ROWS), 0).astype(f32) == rank
    place = jnp.where(place, 1.0, 0.0).astype(bf16)
    pos = jnp.bitwise_and(d_row, ROWS - 1)
    high = jnp.right_shift(pos, 4).astype(f32)
    low = jnp.bitwise_and(pos, 15).astype(f32)
    line = lax.broadcasted_iota(jnp.int32, (88, ROWS), 0)
    extra = jnp.where(line == 0, high, jnp.where(line == 1, low, 0.0))
    ext = jnp.concatenate([xt_ref[...].astype(f32), extra], axis=0).astype(bf16)
    o_ref[...] = lax.dot_general(place, ext, NT, preferred_element_type=f32).astype(bf16)


def front_kernel(
    y_ref, dest_ref, xm_ref, xc_ref, p_ref, w1_ref, b1_ref, w2_ref, b2_ref, w3_ref,
    s_ref, o_ref, q_ref, h1, w2_v, w3_v, acc, sem,
):
    weight_copies(w2_ref, w3_ref, w2_v, w3_v, sem)
    reorder(dest_ref, xm_ref, s_ref)
    for j in range(8):
        q_ref[j * 64 : (j + 1) * 64, :] = p_ref[:, j * 256 : (j + 1) * 256].astype(bf16)
    xc = xc_ref[:, pl.ds(pl.multiple_of(y_ref[0] * UNIT, UNIT), UNIT)]
    x = lax.dot_general(xc, w1_ref[...], TN, preferred_element_type=f32)
    h1[...] = jnp.maximum(x + b1_ref[...], 0.0).astype(bf16)
    last_layers(w2_ref, b2_ref, w3_ref, o_ref, h1, w2_v, w3_v, acc, sem)


def row_kernel(r_ref, w1_ref, b1_ref, w2_ref, b2_ref, w3_ref, o_ref, h1, w2_v, w3_v, acc, sem):
    weight_copies(w2_ref, w3_ref, w2_v, w3_v, sem)
    got = r_ref[...]
    lane = lax.broadcasted_iota(jnp.int32, (8, 128), 1)
    pick = jnp.where(lane == 40, 16.0, jnp.where(lane == 41, 1.0, 0.0)).astype(bf16)
    pos = lax.dot_general(pick, got, NT, preferred_element_type=f32)[0:1, :]
    place = lax.broadcasted_iota(jnp.int32, (ROWS, ROWS), 0).astype(f32) == pos
    place = jnp.where(place, 1.0, 0.0).astype(bf16)
    x = dot(place, got).astype(bf16)[:, :40]
    h1[...] = jnp.maximum(dot(x, w1_ref[...]) + b1_ref[...], 0.0).astype(bf16)
    last_layers(w2_ref, b2_ref, w3_ref, o_ref, h1, w2_v, w3_v, acc, sem)


VM = pl.BlockSpec(memory_space=pltpu.VMEM)
SM = pl.BlockSpec(memory_space=pltpu.SMEM)
HB = pl.BlockSpec(memory_space=pltpu.HBM)
LIMIT = pltpu.CompilerParams(vmem_limit_bytes=22 * 2**20)
WEIGHT_SPECS = [VM, VM, HB, VM, HB]


def net_scratch(m, hid, ft):
    return [
        pltpu.VMEM((m, hid), bf16),
        pltpu.VMEM((hid // CHUNK, hid, CHUNK), bf16),
        pltpu.VMEM((hid, ft), bf16),
        pltpu.VMEM((m, ft), f32),
        pltpu.SemaphoreType.DMA((hid // CHUNK + 1,)),
    ]


def front(y, dest, x_m, x_c, p_t, w1, b1, w2, b2, w3):
    hid, ft = w2.shape[0], w3.shape[1]
    return pl.pallas_call(
        front_kernel,
        in_specs=[SM, VM, VM, VM, VM, *WEIGHT_SPECS],
        out_specs=[VM] * 3,
        out_shape=[
            jax.ShapeDtypeStruct((ROWS, 128), bf16),
            jax.ShapeDtypeStruct((UNIT, ft), bf16),
            jax.ShapeDtypeStruct((UNIT, ft), bf16),
        ],
        scratch_shapes=net_scratch(UNIT, hid, ft),
        name="front",
    )(y, dest.reshape(1, ROWS), x_m, x_c, p_t, w1, b1.reshape(1, -1), w2, b2.reshape(1, -1), w3)


def row_net(got, w1, b1, w2, b2, w3):
    hid, ft = w2.shape[0], w3.shape[1]
    return pl.pallas_call(
        row_kernel,
        in_specs=[VM, *WEIGHT_SPECS],
        out_specs=VM,
        out_shape=jax.ShapeDtypeStruct((ROWS, ft), bf16),
        scratch_shapes=net_scratch(ROWS, hid, ft),
        compiler_params=pltpu.CompilerParams(vmem_limit_bytes=57 * 2**20),
        name="row_net",
    )(got, w1, b1.reshape(1, -1), w2, b2.reshape(1, -1), w3)


def rbf_kernel(off_ref, rel_ref, *refs, nr, pairs, with_init, bm):
    rows, refs = refs[:nr], refs[nr:]
    cols, refs = refs[: 2 * pairs], refs[2 * pairs :]
    if with_init:
        init_ref, refs = refs[0], refs[1:]
    outs, refs = refs[:nr], refs[nr:]
    sc, sqr, sv, kv, acc = refs
    m = nr * ROWS
    rel = rel_ref[...]
    ones = jnp.ones((8, FEAT), bf16)
    for j in range(nr):
        at = slice(j * ROWS, (j + 1) * ROWS)
        rf = rows[j][...].astype(f32)
        sc[at, :] = (rf * (rel * LOG2E)).astype(bf16)
        w = rel * rf * rf
        hi = w.astype(bf16)
        lo = (w - hi.astype(f32)).astype(bf16)
        sqr[:, at] = (-0.5 * LOG2E) * (
            lax.dot_general(ones, hi, NT, preferred_element_type=f32)
            + lax.dot_general(ones, lo, NT, preferred_element_type=f32)
        )
        acc[:, at] = init_ref[...] if with_init else jnp.zeros((64, ROWS), f32)
    for p in range(pairs):
        a_ref, b_ref = cols[2 * p], cols[2 * p + 1]
        blocks = ((a_ref, 0, 512), (a_ref, 1024, 256), (b_ref, 0, 256), (b_ref, 256, 512), (b_ref, 768, 512))
        slot = p % 2
        to = 0
        for ref, at, size in blocks:
            c = ref[at : at + size, :].astype(f32)
            total = jnp.sum(rel * c * c, axis=1, keepdims=True)
            sv[slot, to : to + size, :] = jnp.broadcast_to((-0.5 * LOG2E) * total, (size, 128))
            to += size
        probe = []
        for u in range(4):
            at = pl.multiple_of(512 + off_ref[u] * 128, 128)
            probe += [a_ref[pl.ds(at, 64), :], a_ref[pl.ds(at + 64, 64), :]]
        probe = jnp.concatenate(probe, axis=1)
        for r in range(0, m, bm):
            to = 0
            for ref, at, size in blocks:
                s = lax.dot_general(ref[at : at + size, :], sc[r : r + bm, :], NT, preferred_element_type=f32)
                q = jnp.concatenate([sv[slot, to : to + size, :]] * (bm // 128), axis=1)
                kv[slot, to : to + size, r : r + bm] = jnp.exp2(s + (q + sqr[0:1, r : r + bm])).astype(bf16)
                to += size
            acc[:, r : r + bm] += dot(probe, kv[slot, :, r : r + bm])
    for j in range(nr):
        outs[j][...] = acc[:, j * ROWS : (j + 1) * ROWS].astype(outs[j].dtype)


def rbf(off, rel, rows, col_pairs, init=None, out=f32, bm=256):
    nr, pairs = len(rows), len(col_pairs)
    args = [*rows, *(x for pair in col_pairs for x in pair), *([] if init is None else [init])]
    m = nr * ROWS
    return pl.pallas_call(
        functools.partial(rbf_kernel, nr=nr, pairs=pairs, with_init=init is not None, bm=bm),
        in_specs=[SM, VM] + [VM] * len(args),
        out_specs=[VM] * nr,
        out_shape=[jax.ShapeDtypeStruct((64, ROWS), out)] * nr,
        scratch_shapes=[
            pltpu.VMEM((m, FEAT), bf16),
            pltpu.VMEM((8, m), f32),
            pltpu.VMEM((2, 2048, 128), f32),
            pltpu.VMEM((2, 2048, m), bf16),
            pltpu.VMEM((64, m), f32),
        ],
        compiler_params=LIMIT,
    )(off, rel, *args)


def ring(shift):
    return [(i, (i + shift) % 4) for i in range(4)]


Z = ("zh", "zl")
SWAP = [(0, 1), (1, 0)]


def steps(x_m, dest, x_c, w1, b1, w2, b2, w3, rel, probes):
    rel = rel.reshape(1, FEAT)
    y = lax.axis_index("y").astype(jnp.int32)
    off = jnp.stack([y, (y + 3) % 4, (y + 1) % 4, (y + 2) % 4]).astype(jnp.int32)
    sent, own, probe = front(y.reshape(1), dest, x_m.T, x_c.T, probes.T, w1, b1, w2, b2, w3)
    u1 = lax.ppermute(own, "y", ring(1))
    u3 = lax.ppermute(own, "y", ring(3))
    u2 = lax.ppermute(own, "y", ring(2))
    got = lax.all_to_all(sent, ALL, 0, 0, tiled=True)
    u1, u3, u2, got = lax.optimization_barrier((u1, u3, u2, got))
    feats = row_net(got, w1, b1, w2, b2, w3)
    ca = jnp.concatenate([own, probe, u1[:256]], 0)
    cb = jnp.concatenate([u1[256:], u3, u2], 0)
    za = lax.ppermute(ca, Z, ring(1))
    zb = lax.ppermute(cb, Z, ring(3))
    ca2, cb2, feats = lax.optimization_barrier((ca, cb, feats))
    f1 = lax.ppermute(feats, "x", ring(1))
    f3 = lax.ppermute(feats, "x", ring(3))
    pa = lax.ppermute(ca2, "core", SWAP)
    pb = lax.ppermute(cb2, "core", SWAP)
    near = [(ca, cb), (pa, pb)]
    held = pltpu.with_memory_space_constraint(feats, pltpu.HBM)
    (first,) = rbf(off, rel, [held], near[:1])
    za, zb, first = lax.optimization_barrier((za, zb, first))
    pza = lax.ppermute(za, "core", SWAP)
    pzb = lax.ppermute(zb, "core", SWAP)
    far = [(za, zb), (pza, pzb)]
    (first,) = rbf(off, rel, [feats], near[1:], first)
    f1, f3, first = lax.optimization_barrier((f1, f3, first))
    f2 = lax.ppermute(f1, "x", ring(1))
    t1, t3 = rbf(off, rel, [f1, f3], near + far, out=bf16)
    r1 = lax.ppermute(t1, "x", ring(3))
    r3 = lax.ppermute(t3, "x", ring(1))
    (t2,) = rbf(off, rel, [f2], near + far, out=bf16)
    r2 = lax.ppermute(t2, "x", ring(2))
    (mine,) = rbf(off, rel, [feats], far, first)
    total = mine + r1.astype(f32) + r3.astype(f32) + r2.astype(f32)
    return total.T


def solution(mesh):
    fine = Mesh(mesh.devices.reshape(4, 2, 2, 4, 2), ALL)
    placed = (P(ALL, None), P(ALL), P(COL, None), P(), P(), P(), P(), P(), P(), P(COL, None))
    return jax.shard_map(steps, mesh=fine, in_specs=placed, out_specs=P(ALL, None), check_vma=False)
```
